512 devices in a mesh: rows: 32 (over z, y_hi), cols: 16 (over x, y_lo, core).
Axes of the slice: x: 4, y: 8 (y_hi: 4, y_lo: 2; y = y_hi * 2 + y_lo), z: 8, core: 2. Of those that a mesh axis runs over, the one named last changes fastest.
Arguments:
- adjoint: float32 [3, 128, 384, 256], P(None, 'cols', 'rows'), may hold values from -6 to 6
- base_flow: bfloat16 [3, 128, 384, 256], P(None, 'cols', 'rows'), may hold values from -6 to 6
- stream_pair: bfloat16 [512, 256], replicated, may hold values from -0.375 to 0.375
- normal_pair: bfloat16 [768, 384], replicated, may hold values from -0.3125 to 0.3125
- span_pair: bfloat16 [256, 128], replicated, may hold values from -0.5 to 0.5
Outputs:
- adjoint_next: float32 [3, 128, 384, 256], P(None, 'cols', 'rows')
The draws below stay inside these ranges and needn't reach their ends.
All inputs are finite; a program needn't handle non-finite values.
Results may differ from the reference program's by a relative error of at most 0.0023.
Values may be sent and summed in bfloat16 or wider, within the bound.
No kernel may reach another device: no remote copies, remote signals or barrier semaphores. Data moves between devices by JAX's collectives and lax.ppermute only.
A program may use at most 64 MiB of HBM per device.

```python
import jax
import jax.numpy as jnp
from jax import lax

NX = 256
NY = 384
NZ = 128


def shard_levels(own_key, extent, pieces, smallest, largest):
    level, own = 1.0, jax.random.fold_in(own_key, 6)
    for axis_at, blocks in pieces:
        heights = jnp.exp(jax.random.uniform(jax.random.fold_in(own, axis_at), (blocks,), jnp.float32, smallest / len(pieces), largest / len(pieces)))
        level = level * jnp.repeat(heights, extent[axis_at] // blocks).reshape([-1 if axis == axis_at else 1 for axis in range(len(extent))])
    return level


def bell_draw(stream_key, extent, scale, bound, cuts=(), held_as=jnp.bfloat16):
    values = jax.random.normal(stream_key, extent, jnp.float32) * scale
    if len(cuts) > 0:
        values = shard_levels(stream_key, extent, cuts, -0.22, 0.18) * values
    return jnp.clip(values, min=-bound, max=bound).astype(held_as)


def setup_inputs(seed: int = 0) -> dict:
    seeds = jax.random.split(jax.random.key(seed), 6)
    return {
        "adjoint": bell_draw(seeds[0], (3, NZ, NY, NX), 1.0, 6.0, ((1, 16), (2, 32)), jnp.float32),
        "base_flow": bell_draw(seeds[1], (3, NZ, NY, NX), 1.0, 6.0, ((1, 16), (2, 32))),
        "stream_pair": bell_draw(seeds[2], (2 * NX, NX), NX ** -0.5, 0.375),
        "normal_pair": bell_draw(seeds[3], (2 * NY, NY), NY ** -0.5, 0.3125),
        "span_pair": bell_draw(seeds[4], (2 * NZ, NZ), NZ ** -0.5, 0.5),
    }


viscosity = 0.5
section_step = 0.5


def direction_terms(lines, matrices, axis_index):
    length = lines.shape[3]
    adjoint_f = lines[:3].astype(jnp.float32)
    base_f = lines[3:].astype(jnp.float32)
    matrix_f = matrices.astype(jnp.float32)
    derivs = jnp.einsum("fabn,mn->fabm", adjoint_f, matrix_f, precision=lax.Precision.HIGHEST)
    first_deriv = derivs[..., :length]
    second = derivs[..., length:]
    base_deriv = jnp.einsum("fabn,mn->fabm", base_f, matrix_f[:length], precision=lax.Precision.HIGHEST)
    transfer = jnp.sum(adjoint_f * base_deriv, axis=0)
    result = base_f[axis_index][None] * first_deriv + viscosity * second
    listing = [result[component] - transfer if component == axis_index else result[component] for component in range(3)]
    return jnp.stack(listing)


def reference(adjoint, base_flow, stream_pair, normal_pair, span_pair):
    stacked = jnp.concatenate([adjoint.astype(jnp.bfloat16), base_flow.astype(jnp.bfloat16)], axis=0)

    def along_x(plane):
        return direction_terms(plane[:, None], stream_pair, 0)[:, 0]

    def along_y(plane):
        return direction_terms(plane[:, None], normal_pair, 1)[:, 0]

    def along_z(plane):
        return direction_terms(plane[:, None], span_pair, 2)[:, 0]

    terms_x = lax.map(along_x, stacked.transpose(1, 0, 2, 3)).transpose(1, 0, 2, 3)
    terms_y = lax.map(along_y, stacked.transpose(1, 0, 3, 2)).transpose(1, 0, 3, 2)
    terms_z = lax.map(along_z, stacked.transpose(2, 0, 3, 1)).transpose(1, 3, 0, 2)
    total = terms_x + terms_y + terms_z
    return adjoint + section_step * total
```

```python
import functools

import jax
import jax.numpy as jnp
from jax import lax
from jax.experimental import pallas as pl
from jax.experimental.pallas import tpu as pltpu
from jax.sharding import PartitionSpec as P

viscosity = 0.5
section_step = 0.5
LANES = 128
HALF = 64
PITCH = 40


def left_half(shape):
    return lax.broadcasted_iota(jnp.int32, shape, len(shape) - 1) < HALF


def swap(value):
    return pltpu.roll(value, HALF, value.ndim - 1)


def pack_kernel(a_ref, u_ref, sz_ref, sy_ref, stage):
    comps, y_own, z_own = a_ref.shape[:3]
    left = left_half((y_own, z_own, LANES))
    for j in range(comps):
        for t in range(2):
            a = a_ref[j, :, :, pl.ds(t * LANES, LANES)]
            u = u_ref[j, :, :, pl.ds(t * LANES, LANES)].astype(jnp.float32)
            for h in range(2):
                q = 2 * t + h
                pair = jnp.where(left, a, swap(u)) if h == 0 else jnp.where(left, swap(a), u)
                for group in range(4):
                    sz_ref[group * 4 + q, pl.ds(3 * j, 3)] = pair[3 * group : 3 * group + 3].astype(jnp.bfloat16)
                for y in range(y_own):
                    stage[pl.ds(q * PITCH + j * y_own + y, z_own, stride=4 * PITCH), :] = pair[y]
    rows = comps * y_own
    for p in range(4 * z_own):
        sy_ref[p] = stage[pl.ds(p * PITCH, rows), :].astype(jnp.bfloat16)


def x_kernel(a_ref, u_ref, px_ref, out_ref):
    comps, y_own, z_own, length = a_ref.shape
    rows = y_own * z_own
    px = px_ref[...]
    dims = (((1,), (1,)), ((), ()))
    adjoint = a_ref[...].reshape(comps * rows, length)
    a_b = adjoint.astype(jnp.bfloat16)
    u_f = u_ref[...].astype(jnp.float32).reshape(comps * rows, length)
    derivs = lax.dot_general(a_b, px, dims, preferred_element_type=jnp.float32)
    base_deriv = lax.dot_general(
        u_f.astype(jnp.bfloat16), px[:length], dims, preferred_element_type=jnp.float32
    )
    a_f = a_b.astype(jnp.float32)
    products = a_f * base_deriv
    transfer = products[:rows] + products[rows : 2 * rows] + products[2 * rows :]
    u_dir = u_f[:rows]
    for c in range(comps):
        part = slice(c * rows, (c + 1) * rows)
        term = u_dir * derivs[part, :length] + viscosity * derivs[part, length:]
        if c == 0:
            term = term - transfer
        out_ref[c] = (adjoint[part] + section_step * term).reshape(y_own, z_own, length)


def z_kernel(rz_ref, pz_ref, oz_ref, result):
    peers, slabs, z_own = rz_ref.shape[:3]
    length = peers * z_own
    lines = [rz_ref[:, k].astype(jnp.float32).reshape(length, LANES) for k in range(slabs)]
    packed = jnp.concatenate([v.astype(jnp.bfloat16) for v in lines], axis=1)
    result[...] = jnp.dot(pz_ref[...], packed, preferred_element_type=jnp.float32)
    left = left_half((length, LANES))
    last = []
    for y in range(3):
        vs = [lines[3 * j + y] for j in range(3)]
        ds = [result[:length, pl.ds((3 * j + y) * LANES, LANES)] for j in range(3)]
        ss = [result[length:, pl.ds((3 * j + y) * LANES, LANES)] for j in range(3)]
        u_dir = swap(vs[2])
        transfer = vs[0] * swap(ds[0]) + vs[1] * swap(ds[1]) + vs[2] * swap(ds[2])
        terms = [u_dir * ds[c] + viscosity * ss[c] for c in range(3)]
        last.append(terms[2] - transfer)
        both = jnp.where(left, terms[0], swap(terms[1]))
        oz_ref[:, y] = both.reshape(peers, z_own, LANES).astype(jnp.bfloat16)
    both = jnp.where(left, last[0], swap(last[1]))
    oz_ref[:, 3] = both.reshape(peers, z_own, LANES).astype(jnp.bfloat16)
    oz_ref[:, 4] = last[2].reshape(peers, z_own, LANES).astype(jnp.bfloat16)


def y_kernel(ry_ref, py_ref, oy_ref, stage, lines, result, terms_ref, back):
    peers, rows = ry_ref.shape[:2]
    y_own = rows // 3
    length = peers * y_own
    for p in range(peers):
        stage[pl.ds(p * PITCH, rows), :] = ry_ref[p].astype(jnp.float32)
    for j in range(3):
        for y in range(y_own):
            for g in range(peers // 8):
                lines[j, pl.ds(8 * g * y_own + y, 8, stride=y_own), :] = stage[
                    pl.ds(8 * g * PITCH + j * y_own + y, 8, stride=PITCH), :
                ]
    packed = jnp.concatenate([lines[j].astype(jnp.bfloat16) for j in range(3)], axis=1)
    result[...] = jnp.dot(py_ref[...], packed, preferred_element_type=jnp.float32)
    block = 48
    left = left_half((block, LANES))
    for b in range(length // block):
        at = pl.ds(b * block, block)
        vs = [lines[j, at, :] for j in range(3)]
        ds = [result[at, pl.ds(j * LANES, LANES)] for j in range(3)]
        ss = [result[pl.ds(length + b * block, block), pl.ds(j * LANES, LANES)] for j in range(3)]
        u_dir = swap(vs[1])
        transfer = vs[0] * swap(ds[0]) + vs[1] * swap(ds[1]) + vs[2] * swap(ds[2])
        terms = [u_dir * ds[c] + viscosity * ss[c] for c in range(3)]
        terms_ref[0, at, :] = jnp.where(left, terms[0], swap(terms[1] - transfer))
        terms_ref[1, at, :] = terms[2]
    for h in range(2):
        for y in range(y_own):
            for g in range(peers // 8):
                back[pl.ds(8 * g * 2 * y_own + h * y_own + y, 8, stride=2 * y_own), :] = terms_ref[
                    h, pl.ds(8 * g * y_own + y, 8, stride=y_own), :
                ]
    oy_ref[...] = back[...].reshape(peers, 2 * y_own, LANES).astype(jnp.bfloat16)


def final_kernel(base_ref, rz_ref, ry_ref, out_ref, stage):
    comps, y_own, z_own, _ = base_ref.shape
    left = left_half((z_own, LANES))
    pitch = 2 * y_own
    stage[...] = ry_ref[...].astype(jnp.float32).reshape(stage.shape)

    def y_piece(q, h, y):
        return stage[pl.ds(q * pitch + h * y_own + y, z_own, stride=4 * pitch), :]

    def z_piece(q, y, m):
        return rz_ref[(y // 3) * 4 + q, m].astype(jnp.float32)

    for y in range(y_own):
        w = y % 3
        for t in range(2):
            at = pl.ds(t * LANES, LANES)
            even = y_piece(2 * t, 0, y) + z_piece(2 * t, y, w)
            odd = y_piece(2 * t + 1, 0, y) + z_piece(2 * t + 1, y, w)
            even_last, odd_last = z_piece(2 * t, y, 3 + w // 2), z_piece(2 * t + 1, y, 3 + w // 2)
            if w == 1:
                even_last, odd_last = swap(even_last), swap(odd_last)
            even_last = even_last + y_piece(2 * t, 1, y)
            odd_last = odd_last + y_piece(2 * t + 1, 1, y)
            sums = (
                jnp.where(left, even, swap(odd)),
                jnp.where(left, swap(even), odd),
                jnp.where(left, even_last, swap(odd_last)),
            )
            for c in range(comps):
                out_ref[c, y, :, at] = base_ref[c, y, :, at] + section_step * sums[c]


def local(adjoint, base_flow, stream_pair, normal_pair, span_pair):
    f32, bf16 = jnp.float32, jnp.bfloat16
    rows = lax.axis_size("rows")
    cols = lax.axis_size("cols")
    comps, z_own, y_own, length_x = adjoint.shape
    length_y = rows * y_own
    length_z = cols * z_own
    a = adjoint.transpose(0, 2, 1, 3)
    u = base_flow.transpose(0, 2, 1, 3)
    shape = jax.ShapeDtypeStruct
    exchange = functools.partial(lax.all_to_all, split_axis=0, concat_axis=0, tiled=True)

    send_z, send_y = pl.pallas_call(
        pack_kernel,
        name="pack",
        out_shape=(
            shape((cols, 3 * comps, z_own, LANES), bf16),
            shape((rows, comps * y_own, LANES), bf16),
        ),
        scratch_shapes=[pltpu.VMEM((rows * PITCH, LANES), f32)],
    )(a, u)
    with jax.named_scope("z_out"):
        recv_z = exchange(send_z, "cols")
    with jax.named_scope("y_out"):
        recv_y = exchange(send_y, "rows")
    base = pl.pallas_call(
        x_kernel, name="x_terms", out_shape=shape(a.shape, f32)
    )(a, u, stream_pair)
    terms_z = pl.pallas_call(
        z_kernel,
        name="z_terms",
        out_shape=shape((cols, 5, z_own, LANES), bf16),
        scratch_shapes=[pltpu.VMEM((2 * length_z, 3 * comps * LANES), f32)],
    )(recv_z, span_pair)
    with jax.named_scope("z_back"):
        back_z = exchange(terms_z, "cols")
    terms_y = pl.pallas_call(
        y_kernel,
        name="y_terms",
        out_shape=shape((rows, 2 * y_own, LANES), bf16),
        scratch_shapes=[
            pltpu.VMEM((rows * PITCH, LANES), f32),
            pltpu.VMEM((comps, length_y, LANES), f32),
            pltpu.VMEM((2 * length_y, comps * LANES), f32),
            pltpu.VMEM((2, length_y, LANES), f32),
            pltpu.VMEM((rows * 2 * y_own, LANES), f32),
        ],
    )(recv_y, normal_pair)
    with jax.named_scope("y_back"):
        back_y = exchange(terms_y, "rows")
    out = pl.pallas_call(
        final_kernel,
        name="final",
        out_shape=shape(a.shape, f32),
        scratch_shapes=[pltpu.VMEM((rows * 2 * y_own, LANES), f32)],
    )(base, back_z, back_y)
    return out.transpose(0, 2, 1, 3)


def solution(mesh):
    placed = (P(None, "cols", "rows", None), P(None, "cols", "rows", None), P(), P(), P())
    return jax.shard_map(
        local, mesh=mesh, in_specs=placed, out_specs=P(None, "cols", "rows", None), check_vma=False
    )
```

```python
import functools

import jax
import jax.numpy as jnp
from jax import lax
from jax.experimental import pallas as pl
from jax.experimental.pallas import tpu as pltpu
from jax.sharding import PartitionSpec as P

viscosity = 0.5
section_step = 0.5
LANES = 128
HALF = 64
PITCH = 40


def left_half(shape):
    return lax.broadcasted_iota(jnp.int32, shape, len(shape) - 1) < HALF


def swap(value):
    return pltpu.roll(value, HALF, value.ndim - 1)


def pair_up(a_ref, u_ref, j, t, h, left):
    at = pl.ds(t * LANES, LANES)
    a = a_ref[j, :, :, at]
    u = u_ref[j, :, :, at].astype(jnp.float32)
    return jnp.where(left, a, swap(u)) if h == 0 else jnp.where(left, swap(a), u)


def pack_z_kernel(a_ref, u_ref, sz_ref):
    comps, y_own, z_own = a_ref.shape[:3]
    left = left_half((y_own, z_own, LANES))
    for j in range(comps):
        for q in range(4):
            pair = pair_up(a_ref, u_ref, j, q // 2, q % 2, left).astype(jnp.bfloat16)
            for group in range(4):
                sz_ref[group * 4 + q, pl.ds(3 * j, 3)] = pair[3 * group : 3 * group + 3]


def pack_y_kernel(a_ref, u_ref, sy_ref, stage):
    comps, y_own, z_own = a_ref.shape[:3]
    left = left_half((y_own, z_own, LANES))
    for j in range(comps):
        for q in range(4):
            pair = pair_up(a_ref, u_ref, j, q // 2, q % 2, left)
            for y in range(y_own):
                stage[pl.ds(q * PITCH + j * y_own + y, z_own, stride=4 * PITCH), :] = pair[y]
    rows = comps * y_own
    for p in range(4 * z_own):
        sy_ref[p] = stage[pl.ds(p * PITCH, rows), :].astype(jnp.bfloat16)


def spread(even, odd, even_last, odd_last, left):
    return (
        jnp.where(left, even, swap(odd)),
        jnp.where(left, swap(even), odd),
        jnp.where(left, even_last, swap(odd_last)),
    )


def x_kernel(a_ref, u_ref, px_ref, rz_ref, out_ref):
    comps, y_own, z_own, length = a_ref.shape
    rows = y_own * z_own
    px = px_ref[...]
    dims = (((1,), (1,)), ((), ()))
    adjoint = a_ref[...].reshape(comps * rows, length)
    a_b = adjoint.astype(jnp.bfloat16)
    u_f = u_ref[...].astype(jnp.float32).reshape(comps * rows, length)
    derivs = lax.dot_general(a_b, px, dims, preferred_element_type=jnp.float32)
    base_deriv = lax.dot_general(
        u_f.astype(jnp.bfloat16), px[:length], dims, preferred_element_type=jnp.float32
    )
    a_f = a_b.astype(jnp.float32)
    products = a_f * base_deriv
    transfer = products[:rows] + products[rows : 2 * rows] + products[2 * rows :]
    u_dir = u_f[:rows]
    for c in range(comps):
        part = slice(c * rows, (c + 1) * rows)
        term = u_dir * derivs[part, :length] + viscosity * derivs[part, length:]
        if c == 0:
            term = term - transfer
        out_ref[c] = (adjoint[part] + section_step * term).reshape(y_own, z_own, length)
    left = left_half((z_own, LANES))

    def z_piece(q, y, m):
        return rz_ref[(y // 3) * 4 + q, m].astype(jnp.float32)

    for y in range(y_own):
        w = y % 3
        for t in range(2):
            at = pl.ds(t * LANES, LANES)
            even, odd = z_piece(2 * t, y, w), z_piece(2 * t + 1, y, w)
            even_last, odd_last = z_piece(2 * t, y, 3 + w // 2), z_piece(2 * t + 1, y, 3 + w // 2)
            if w == 1:
                even_last, odd_last = swap(even_last), swap(odd_last)
            sums = spread(even, odd, even_last, odd_last, left)
            for c in range(comps):
                out_ref[c, y, :, at] += section_step * sums[c]


def z_kernel(rz_ref, pz_ref, oz_ref, result):
    peers, slabs, z_own = rz_ref.shape[:3]
    length = peers * z_own
    lines = [rz_ref[:, k].astype(jnp.float32).reshape(length, LANES) for k in range(slabs)]
    packed = jnp.concatenate([v.astype(jnp.bfloat16) for v in lines], axis=1)
    result[...] = jnp.dot(pz_ref[...], packed, preferred_element_type=jnp.float32)
    left = left_half((length, LANES))
    last = []
    for y in range(3):
        vs = [lines[3 * j + y] for j in range(3)]
        ds = [result[:length, pl.ds((3 * j + y) * LANES, LANES)] for j in range(3)]
        ss = [result[length:, pl.ds((3 * j + y) * LANES, LANES)] for j in range(3)]
        u_dir = swap(vs[2])
        transfer = vs[0] * swap(ds[0]) + vs[1] * swap(ds[1]) + vs[2] * swap(ds[2])
        terms = [u_dir * ds[c] + viscosity * ss[c] for c in range(3)]
        last.append(terms[2] - transfer)
        both = jnp.where(left, terms[0], swap(terms[1]))
        oz_ref[:, y] = both.reshape(peers, z_own, LANES).astype(jnp.bfloat16)
    both = jnp.where(left, last[0], swap(last[1]))
    oz_ref[:, 3] = both.reshape(peers, z_own, LANES).astype(jnp.bfloat16)
    oz_ref[:, 4] = last[2].reshape(peers, z_own, LANES).astype(jnp.bfloat16)


def y_kernel(ry_ref, py_ref, oy_ref, stage, lines, result, terms_ref, back):
    peers, rows = ry_ref.shape[:2]
    y_own = rows // 3
    length = peers * y_own
    for p in range(peers):
        stage[pl.ds(p * PITCH, rows), :] = ry_ref[p].astype(jnp.float32)
    for j in range(3):
        for y in range(y_own):
            for g in range(peers // 8):
                lines[j, pl.ds(8 * g * y_own + y, 8, stride=y_own), :] = stage[
                    pl.ds(8 * g * PITCH + j * y_own + y, 8, stride=PITCH), :
                ]
    packed = jnp.concatenate([lines[j].astype(jnp.bfloat16) for j in range(3)], axis=1)
    result[...] = jnp.dot(py_ref[...], packed, preferred_element_type=jnp.float32)
    block = 48
    left = left_half((block, LANES))
    for b in range(length // block):
        at = pl.ds(b * block, block)
        vs = [lines[j, at, :] for j in range(3)]
        ds = [result[at, pl.ds(j * LANES, LANES)] for j in range(3)]
        ss = [result[pl.ds(length + b * block, block), pl.ds(j * LANES, LANES)] for j in range(3)]
        u_dir = swap(vs[1])
        transfer = vs[0] * swap(ds[0]) + vs[1] * swap(ds[1]) + vs[2] * swap(ds[2])
        terms = [u_dir * ds[c] + viscosity * ss[c] for c in range(3)]
        terms_ref[0, at, :] = jnp.where(left, terms[0], swap(terms[1] - transfer))
        terms_ref[1, at, :] = terms[2]
    for h in range(2):
        for y in range(y_own):
            for g in range(peers // 8):
                back[pl.ds(8 * g * 2 * y_own + h * y_own + y, 8, stride=2 * y_own), :] = terms_ref[
                    h, pl.ds(8 * g * y_own + y, 8, stride=y_own), :
                ]
    oy_ref[...] = back[...].reshape(peers, 2 * y_own, LANES).astype(jnp.bfloat16)


def final_kernel(base_ref, ry_ref, out_ref, stage):
    comps, y_own, z_own, _ = base_ref.shape
    left = left_half((z_own, LANES))
    pitch = 2 * y_own
    stage[...] = ry_ref[...].astype(jnp.float32).reshape(stage.shape)

    def y_piece(q, h, y):
        return stage[pl.ds(q * pitch + h * y_own + y, z_own, stride=4 * pitch), :]

    for y in range(y_own):
        for t in range(2):
            at = pl.ds(t * LANES, LANES)
            sums = spread(
                y_piece(2 * t, 0, y), y_piece(2 * t + 1, 0, y), y_piece(2 * t, 1, y), y_piece(2 * t + 1, 1, y), left
            )
            for c in range(comps):
                out_ref[c, y, :, at] = base_ref[c, y, :, at] + section_step * sums[c]


def local(adjoint, base_flow, stream_pair, normal_pair, span_pair):
    f32, bf16 = jnp.float32, jnp.bfloat16
    rows = lax.axis_size("rows")
    cols = lax.axis_size("cols")
    comps, z_own, y_own, length_x = adjoint.shape
    length_y = rows * y_own
    length_z = cols * z_own
    a = adjoint.transpose(0, 2, 1, 3)
    u = base_flow.transpose(0, 2, 1, 3)
    shape = jax.ShapeDtypeStruct
    exchange = functools.partial(lax.all_to_all, split_axis=0, concat_axis=0, tiled=True)

    near = functools.partial(pltpu.with_memory_space_constraint, memory_space=pltpu.VMEM)

    send_z = pl.pallas_call(
        pack_z_kernel, name="pack_z", out_shape=shape((cols, 3 * comps, z_own, LANES), bf16)
    )(a, u)
    send_y = pl.pallas_call(
        pack_y_kernel,
        name="pack_y",
        out_shape=shape((rows, comps * y_own, LANES), bf16),
        scratch_shapes=[pltpu.VMEM((rows * PITCH, LANES), f32)],
    )(a, u)
    with jax.named_scope("z_out"):
        recv_z = exchange(send_z, "cols")
    with jax.named_scope("y_out"):
        recv_y = exchange(send_y, "rows")
    terms_z = pl.pallas_call(
        z_kernel,
        name="z_terms",
        out_shape=shape((cols, 5, z_own, LANES), bf16),
        scratch_shapes=[pltpu.VMEM((2 * length_z, 3 * comps * LANES), f32)],
    )(near(recv_z), span_pair)
    with jax.named_scope("z_back"):
        back_z = exchange(terms_z, "cols")
    terms_y = pl.pallas_call(
        y_kernel,
        name="y_terms",
        out_shape=shape((rows, 2 * y_own, LANES), bf16),
        scratch_shapes=[
            pltpu.VMEM((rows * PITCH, LANES), f32),
            pltpu.VMEM((comps, length_y, LANES), f32),
            pltpu.VMEM((2 * length_y, comps * LANES), f32),
            pltpu.VMEM((2, length_y, LANES), f32),
            pltpu.VMEM((rows * 2 * y_own, LANES), f32),
        ],
    )(near(recv_y), normal_pair)
    with jax.named_scope("y_back"):
        back_y = exchange(terms_y, "rows")
    base = pl.pallas_call(x_kernel, name="x_terms", out_shape=pltpu.VMEM(a.shape, f32))(
        a, u, stream_pair, near(back_z)
    )
    out = pl.pallas_call(
        final_kernel,
        name="final",
        out_shape=shape(a.shape, f32),
        scratch_shapes=[pltpu.VMEM((rows * 2 * y_own, LANES), f32)],
    )(near(base), near(back_y))
    return out.transpose(0, 2, 1, 3)


def solution(mesh):
    placed = (P(None, "cols", "rows", None), P(None, "cols", "rows", None), P(), P(), P())
    return jax.shard_map(
        local, mesh=mesh, in_specs=placed, out_specs=P(None, "cols", "rows", None), check_vma=False
    )
```

```python
import functools

import jax
import jax.numpy as jnp
from jax import lax
from jax.experimental import pallas as pl
from jax.experimental.pallas import tpu as pltpu
from jax.sharding import PartitionSpec as P

viscosity = 0.5
section_step = 0.5
LANES = 128
BACK = 40


def fields(a_ref, u_ref, f, half):
    at = pl.ds(half * LANES, LANES)
    if f < 3:
        return a_ref[f, :, :, at]
    return u_ref[f - 3, :, :, at].astype(jnp.float32)


def pack_y(a_ref, u_ref, out_ref, stage):
    y_own, z_own = a_ref.shape[1:3]
    rows = 6 * y_own
    for f in range(6):
        for half in range(2):
            value = fields(a_ref, u_ref, f, half)
            for y in range(y_own):
                stage[pl.ds(half * rows + f * y_own + y, z_own, stride=2 * rows), :] = value[y]
    out_ref[...] = stage[...].reshape(2 * z_own, rows, LANES).astype(jnp.bfloat16)


def pack_z(a_ref, u_ref, out_ref):
    y_own, z_own = a_ref.shape[1:3]
    for f in range(6):
        for half in range(2):
            value = fields(a_ref, u_ref, f, half).astype(jnp.bfloat16)
            for y in range(y_own):
                row = ((y // 3 * 2 + half) * 18 + f * 3 + y % 3) * z_own
                out_ref[row // 72, pl.ds(row % 72, z_own), :] = value[y]


def pack_kernel(y_core, a_ref, u_ref, out_ref, stage):
    is_y = lax.axis_index("cols") % 2 == y_core

    @pl.when(is_y)
    def _():
        pack_y(a_ref, u_ref, out_ref, stage)

    @pl.when(jnp.logical_not(is_y))
    def _():
        pack_z(a_ref, u_ref, out_ref)


def x_kernel(a_ref, u_ref, px_ref, out_ref):
    comps, y_own, z_own, length = a_ref.shape
    rows = y_own * z_own
    px = px_ref[...]
    dims = (((1,), (1,)), ((), ()))
    adjoint = a_ref[...].reshape(comps * rows, length)
    a_b = adjoint.astype(jnp.bfloat16)
    u_f = u_ref[...].astype(jnp.float32).reshape(comps * rows, length)
    derivs = lax.dot_general(a_b, px, dims, preferred_element_type=jnp.float32)
    base_deriv = lax.dot_general(
        u_f.astype(jnp.bfloat16), px[:length], dims, preferred_element_type=jnp.float32
    )
    products = a_b.astype(jnp.float32) * base_deriv
    transfer = products[:rows] + products[rows : 2 * rows] + products[2 * rows :]
    u_dir = u_f[:rows]
    for c in range(comps):
        part = slice(c * rows, (c + 1) * rows)
        term = u_dir * derivs[part, :length] + viscosity * derivs[part, length:]
        if c == 0:
            term = term - transfer
        out_ref[c] = (adjoint[part] + section_step * term).reshape(y_own, z_own, length)


def z_kernel(rz_ref, pz_ref, oz_ref, derivs, base_derivs):
    chips, _, slabs, z_own = rz_ref.shape[:4]
    length = chips * 2 * z_own
    lines = [rz_ref[:, :, k].astype(jnp.float32).reshape(length, LANES) for k in range(slabs)]
    packed = [v.astype(jnp.bfloat16) for v in lines]
    pz = pz_ref[...]
    derivs[...] = jnp.dot(pz, jnp.concatenate(packed[:9], axis=1), preferred_element_type=jnp.float32)
    base_derivs[...] = jnp.dot(
        pz[:length], jnp.concatenate(packed[9:], axis=1), preferred_element_type=jnp.float32
    )
    for y in range(3):
        at = [pl.ds((3 * j + y) * LANES, LANES) for j in range(3)]
        u_dir = lines[9 + 3 * 2 + y]
        transfer = sum(lines[3 * j + y] * base_derivs[:, at[j]] for j in range(3))
        for c in range(3):
            term = u_dir * derivs[:length, at[c]] + viscosity * derivs[length:, at[c]]
            if c == 2:
                term = term - transfer
            oz_ref[:, :, 3 * c + y] = term.reshape(chips, 2, z_own, LANES).astype(jnp.bfloat16)


def y_kernel(ry_ref, py_ref, oy_ref, stage, lines, derivs, base_derivs, terms, back):
    peers, rows = ry_ref.shape[:2]
    y_own = rows // 6
    length = peers * y_own
    stage[...] = ry_ref[...].astype(jnp.float32).reshape(stage.shape)
    for f in range(6):
        for y in range(y_own):
            for g in range(peers // 8):
                lines[f, pl.ds(8 * g * y_own + y, 8, stride=y_own), :] = stage[
                    pl.ds(8 * g * rows + f * y_own + y, 8, stride=rows), :
                ]
    packed = [lines[f].astype(jnp.bfloat16) for f in range(6)]
    derivs[...] = jnp.dot(
        py_ref[...], jnp.concatenate(packed[:3], axis=1), preferred_element_type=jnp.float32
    )
    base_derivs[...] = jnp.dot(
        py_ref[pl.ds(0, length), :], jnp.concatenate(packed[3:], axis=1), preferred_element_type=jnp.float32
    )
    block = 48
    for b in range(length // block):
        at = pl.ds(b * block, block)
        lane = [pl.ds(j * LANES, LANES) for j in range(3)]
        u_dir = lines[4, at, :]
        transfer = sum(lines[j, at, :] * base_derivs[at, lane[j]] for j in range(3))
        for c in range(3):
            term = u_dir * derivs[at, lane[c]] + viscosity * derivs[pl.ds(length + b * block, block), lane[c]]
            if c == 1:
                term = term - transfer
            terms[c, at, :] = term
    for c in range(3):
        for y in range(y_own):
            for g in range(peers // 8):
                back[pl.ds(8 * g * BACK + c * y_own + y, 8, stride=BACK), :] = terms[
                    c, pl.ds(8 * g * y_own + y, 8, stride=y_own), :
                ]
    for p in range(peers):
        used = 3 * y_own
        back[pl.ds(p * BACK + used, BACK - used), :] = jnp.zeros((BACK - used, LANES), jnp.float32)
    oy_ref[...] = back[...].reshape(peers, BACK, LANES).astype(jnp.bfloat16)


def order_kernel(rz_ref, out_ref):
    pieces, _, slabs, z_own = rz_ref.shape[:4]
    for side in range(2):
        for p in range(pieces):
            for k in range(slabs):
                row = (p * slabs + k) * z_own
                out_ref[16 * side + row // BACK, pl.ds(row % BACK, z_own), :] = rz_ref[p, 1 - side, k]
        for row in range(pieces * slabs * z_own, 16 * BACK, z_own):
            out_ref[16 * side + row // BACK, pl.ds(row % BACK, z_own), :] = jnp.zeros((z_own, LANES), jnp.bfloat16)


def add_kernel(y_core, base_ref, part_ref, out_ref, stage):
    comps, y_own, z_own, _ = base_ref.shape
    is_y = lax.axis_index("cols") % 2 == y_core

    @pl.when(is_y)
    def _():
        stage[...] = part_ref[pl.ds(0, 16)].astype(jnp.float32).reshape(stage.shape)
        for c in range(comps):
            for y in range(y_own):
                for half in range(2):
                    at = pl.ds(half * LANES, LANES)
                    piece = stage[pl.ds(half * BACK + c * y_own + y, z_own, stride=2 * BACK), :]
                    out_ref[c, y, :, at] = base_ref[c, y, :, at] + section_step * piece

    @pl.when(jnp.logical_not(is_y))
    def _():
        for c in range(comps):
            for y in range(y_own):
                for half in range(2):
                    at = pl.ds(half * LANES, LANES)
                    row = ((y // 3 * 2 + half) * 9 + c * 3 + y % 3) * z_own
                    piece = part_ref[row // BACK, pl.ds(row % BACK, z_own), :].astype(jnp.float32)
                    out_ref[c, y, :, at] = base_ref[c, y, :, at] + section_step * piece


def local(adjoint, base_flow, stream_pair, normal_pair, span_pair):
    f32, bf16 = jnp.float32, jnp.bfloat16
    rows = lax.axis_size("rows")
    cols = lax.axis_size("cols")
    chips = cols // 2
    _, z_own, y_own, length_x = adjoint.shape
    length_y = rows * y_own
    length_z = cols * z_own
    a = adjoint.transpose(0, 2, 1, 3)
    u = base_flow.transpose(0, 2, 1, 3)
    shape = jax.ShapeDtypeStruct
    near = functools.partial(pltpu.with_memory_space_constraint, memory_space=pltpu.VMEM)
    exchange = functools.partial(lax.all_to_all, split_axis=0, concat_axis=0, tiled=True)
    partner = [(i, i ^ 1) for i in range(cols)]
    alike = [list(range(core, cols, 2)) for core in range(2)]

    def pack(y_core, name):
        return pl.pallas_call(
            functools.partial(pack_kernel, y_core),
            name=name,
            out_shape=shape((2 * z_own, 6 * y_own, LANES), bf16),
            scratch_shapes=[pltpu.VMEM((2 * z_own * 6 * y_own, LANES), f32)],
        )(a, u)

    def x_terms():
        return pl.pallas_call(x_kernel, name="x_terms", out_shape=shape(a.shape, f32))(a, u, stream_pair)

    def add(y_core, name, base, part, near_base):
        return pl.pallas_call(
            functools.partial(add_kernel, y_core),
            name=name,
            out_shape=near_base(a.shape, f32),
            scratch_shapes=[pltpu.VMEM((16 * BACK, LANES), f32)],
        )(base, near(part))

    def along_y(keep, recv):
        base = x_terms()
        lines = exchange(jnp.concatenate([keep, recv], axis=0), "rows")
        terms = pl.pallas_call(
            y_kernel,
            name="y_terms",
            out_shape=shape((rows, BACK, LANES), bf16),
            scratch_shapes=[
                pltpu.VMEM((rows * 6 * y_own, LANES), f32),
                pltpu.VMEM((6, length_y, LANES), f32),
                pltpu.VMEM((2 * length_y, 3 * LANES), f32),
                pltpu.VMEM((length_y, 3 * LANES), f32),
                pltpu.VMEM((3, length_y, LANES), f32),
                pltpu.VMEM((rows * BACK, LANES), f32),
            ],
        )(near(lines), normal_pair)
        return exchange(terms, "rows"), base

    def along_z(keep, recv):
        base = x_terms()
        pair = [part.reshape(chips, 1, 18, z_own, LANES) for part in (recv, keep)]
        lines = exchange(jnp.concatenate(pair, axis=1), "cols", axis_index_groups=alike)
        terms = pl.pallas_call(
            z_kernel,
            name="z_terms",
            out_shape=shape((chips, 2, 9, z_own, LANES), bf16),
            scratch_shapes=[
                pltpu.VMEM((2 * length_z, 9 * LANES), f32),
                pltpu.VMEM((length_z, 9 * LANES), f32),
            ],
        )(lines, span_pair)
        back = exchange(terms, "cols", axis_index_groups=alike)
        ordered = pl.pallas_call(
            order_kernel, name="order_z", out_shape=shape((rows, BACK, LANES), bf16)
        )(back)
        return ordered, base

    core = lax.axis_index("cols") % 2
    recv = lax.ppermute(pack(1, "pack_send"), "cols", partner)
    keep = pack(0, "pack_keep")
    both, base = lax.cond(core == 0, along_y, along_z, keep, recv)
    other = lax.ppermute(both[rows // 2 :], "cols", partner)
    base = add(0, "add_own", base, both, pltpu.VMEM)
    out = add(1, "add_other", near(base), other, shape)
    return out.transpose(0, 2, 1, 3)


def solution(mesh):
    placed = (P(None, "cols", "rows", None), P(None, "cols", "rows", None), P(), P(), P())
    return jax.shard_map(
        local, mesh=mesh, in_specs=placed, out_specs=P(None, "cols", "rows", None), check_vma=False
    )
```

```python
import functools

import jax
import jax.numpy as jnp
from jax import lax
from jax.experimental import pallas as pl
from jax.experimental.pallas import tpu as pltpu
from jax.sharding import PartitionSpec as P

viscosity = 0.5
section_step = 0.5
LANES = 128
BACK = 40


def fields(a_ref, u_ref, f, half):
    at = pl.ds(half * LANES, LANES)
    if f < 3:
        return a_ref[f, :, :, at]
    return u_ref[f - 3, :, :, at].astype(jnp.float32)


def pack_y(a_ref, u_ref, out_ref, stage):
    y_own, z_own = a_ref.shape[1:3]
    rows = 6 * y_own
    for f in range(6):
        for half in range(2):
            value = fields(a_ref, u_ref, f, half)
            for y in range(y_own):
                stage[pl.ds(half * rows + f * y_own + y, z_own, stride=2 * rows), :] = value[y]
    out_ref[...] = stage[...].reshape(2 * z_own, rows, LANES).astype(jnp.bfloat16)


def pack_z(a_ref, u_ref, out_ref):
    y_own, z_own = a_ref.shape[1:3]
    for f in range(6):
        for half in range(2):
            value = fields(a_ref, u_ref, f, half).astype(jnp.bfloat16)
            for y in range(y_own):
                row = ((y // 3 * 2 + half) * 18 + f * 3 + y % 3) * z_own
                out_ref[row // 72, pl.ds(row % 72, z_own), :] = value[y]


def pack_kernel(y_core, a_ref, u_ref, out_ref, stage):
    is_y = lax.axis_index("cols") % 2 == y_core

    @pl.when(is_y)
    def _():
        pack_y(a_ref, u_ref, out_ref, stage)

    @pl.when(jnp.logical_not(is_y))
    def _():
        pack_z(a_ref, u_ref, out_ref)


def x_kernel(a_ref, u_ref, px_ref, out_ref):
    comps, y_own, z_own, length = a_ref.shape
    rows = y_own * z_own
    px = px_ref[...]
    dims = (((1,), (1,)), ((), ()))
    adjoint = a_ref[...].reshape(comps * rows, length)
    a_b = adjoint.astype(jnp.bfloat16)
    u_f = u_ref[...].astype(jnp.float32).reshape(comps * rows, length)
    derivs = lax.dot_general(a_b, px, dims, preferred_element_type=jnp.float32)
    base_deriv = lax.dot_general(
        u_f.astype(jnp.bfloat16), px[:length], dims, preferred_element_type=jnp.float32
    )
    products = a_b.astype(jnp.float32) * base_deriv
    transfer = products[:rows] + products[rows : 2 * rows] + products[2 * rows :]
    u_dir = u_f[:rows]
    for c in range(comps):
        part = slice(c * rows, (c + 1) * rows)
        term = u_dir * derivs[part, :length] + viscosity * derivs[part, length:]
        if c == 0:
            term = term - transfer
        out_ref[c] = (adjoint[part] + section_step * term).reshape(y_own, z_own, length)


def z_kernel(rz_ref, pz_ref, oz_ref, derivs, base_derivs):
    chips, _, slabs, z_own = rz_ref.shape[:4]
    length = chips * 2 * z_own
    lines = [rz_ref[:, :, k].astype(jnp.float32).reshape(length, LANES) for k in range(slabs)]
    packed = [v.astype(jnp.bfloat16) for v in lines]
    pz = pz_ref[...]
    derivs[...] = jnp.dot(pz, jnp.concatenate(packed[:9], axis=1), preferred_element_type=jnp.float32)
    base_derivs[...] = jnp.dot(
        pz[:length], jnp.concatenate(packed[9:], axis=1), preferred_element_type=jnp.float32
    )
    for y in range(3):
        at = [pl.ds((3 * j + y) * LANES, LANES) for j in range(3)]
        u_dir = lines[9 + 3 * 2 + y]
        transfer = sum(lines[3 * j + y] * base_derivs[:, at[j]] for j in range(3))
        for c in range(3):
            term = u_dir * derivs[:length, at[c]] + viscosity * derivs[length:, at[c]]
            if c == 2:
                term = term - transfer
            oz_ref[:, :, 3 * c + y] = term.reshape(chips, 2, z_own, LANES).astype(jnp.bfloat16)


def y_kernel(ry_ref, py_ref, oy_ref, stage, lines, derivs, base_derivs, terms, back):
    peers, rows = ry_ref.shape[:2]
    y_own = rows // 6
    length = peers * y_own
    stage[...] = ry_ref[...].astype(jnp.float32).reshape(stage.shape)
    for f in range(6):
        for y in range(y_own):
            for g in range(peers // 8):
                lines[f, pl.ds(8 * g * y_own + y, 8, stride=y_own), :] = stage[
                    pl.ds(8 * g * rows + f * y_own + y, 8, stride=rows), :
                ]
    packed = [lines[f].astype(jnp.bfloat16) for f in range(6)]
    derivs[...] = jnp.dot(
        py_ref[...], jnp.concatenate(packed[:3], axis=1), preferred_element_type=jnp.float32
    )
    base_derivs[...] = jnp.dot(
        py_ref[pl.ds(0, length), :], jnp.concatenate(packed[3:], axis=1), preferred_element_type=jnp.float32
    )
    block = 48
    for b in range(length // block):
        at = pl.ds(b * block, block)
        lane = [pl.ds(j * LANES, LANES) for j in range(3)]
        u_dir = lines[4, at, :]
        transfer = sum(lines[j, at, :] * base_derivs[at, lane[j]] for j in range(3))
        for c in range(3):
            term = u_dir * derivs[at, lane[c]] + viscosity * derivs[pl.ds(length + b * block, block), lane[c]]
            if c == 1:
                term = term - transfer
            terms[c, at, :] = term
    for c in range(3):
        for y in range(y_own):
            for g in range(peers // 8):
                back[pl.ds(8 * g * BACK + c * y_own + y, 8, stride=BACK), :] = terms[
                    c, pl.ds(8 * g * y_own + y, 8, stride=y_own), :
                ]
    for p in range(peers):
        used = 3 * y_own
        back[pl.ds(p * BACK + used, BACK - used), :] = jnp.zeros((BACK - used, LANES), jnp.float32)
    oy_ref[...] = back[...].reshape(peers, BACK, LANES).astype(jnp.bfloat16)


def order_kernel(rz_ref, out_ref):
    pieces, _, slabs, z_own = rz_ref.shape[:4]
    for side in range(2):
        for p in range(pieces):
            for k in range(slabs):
                row = (p * slabs + k) * z_own
                out_ref[16 * side + row // BACK, pl.ds(row % BACK, z_own), :] = rz_ref[p, 1 - side, k]
        for row in range(pieces * slabs * z_own, 16 * BACK, z_own):
            out_ref[16 * side + row // BACK, pl.ds(row % BACK, z_own), :] = jnp.zeros((z_own, LANES), jnp.bfloat16)


def add_kernel(y_core, base_ref, part_ref, out_ref, stage):
    comps, y_own, z_own, _ = base_ref.shape
    is_y = lax.axis_index("cols") % 2 == y_core

    @pl.when(is_y)
    def _():
        stage[...] = part_ref[pl.ds(0, 16)].astype(jnp.float32).reshape(stage.shape)
        for c in range(comps):
            for y in range(y_own):
                for half in range(2):
                    at = pl.ds(half * LANES, LANES)
                    piece = stage[pl.ds(half * BACK + c * y_own + y, z_own, stride=2 * BACK), :]
                    out_ref[c, y, :, at] = base_ref[c, y, :, at] + section_step * piece

    @pl.when(jnp.logical_not(is_y))
    def _():
        for c in range(comps):
            for y in range(y_own):
                for half in range(2):
                    at = pl.ds(half * LANES, LANES)
                    row = ((y // 3 * 2 + half) * 9 + c * 3 + y % 3) * z_own
                    piece = part_ref[row // BACK, pl.ds(row % BACK, z_own), :].astype(jnp.float32)
                    out_ref[c, y, :, at] = base_ref[c, y, :, at] + section_step * piece


def local(adjoint, base_flow, stream_pair, normal_pair, span_pair):
    f32, bf16 = jnp.float32, jnp.bfloat16
    rows = lax.axis_size("rows")
    cols = lax.axis_size("cols")
    chips = cols // 2
    _, z_own, y_own, length_x = adjoint.shape
    length_y = rows * y_own
    length_z = cols * z_own
    a = adjoint.transpose(0, 2, 1, 3)
    u = base_flow.transpose(0, 2, 1, 3)
    local_shape = pltpu.VMEM
    near = functools.partial(pltpu.with_memory_space_constraint, memory_space=pltpu.VMEM)
    exchange = functools.partial(lax.all_to_all, split_axis=0, concat_axis=0, tiled=True)
    partner = [(i, i ^ 1) for i in range(cols)]
    alike = [list(range(core, cols, 2)) for core in range(2)]

    def pack(y_core, name, place):
        return pl.pallas_call(
            functools.partial(pack_kernel, y_core),
            name=name,
            out_shape=local_shape((2 * z_own, 6 * y_own, LANES), bf16),
            scratch_shapes=[pltpu.VMEM((2 * z_own * 6 * y_own, LANES), f32)],
        )(place(a), place(u))

    def x_terms():
        return pl.pallas_call(x_kernel, name="x_terms", out_shape=local_shape(a.shape, f32))(
            near(a), near(u), near(stream_pair)
        )

    def add(y_core, name, base, part, shape):
        return pl.pallas_call(
            functools.partial(add_kernel, y_core),
            name=name,
            out_shape=shape(a.shape, f32),
            scratch_shapes=[pltpu.VMEM((16 * BACK, LANES), f32)],
        )(near(base), near(part))

    def along_y(keep, recv):
        lines = exchange(jnp.concatenate([keep, recv], axis=0), "rows")
        terms = pl.pallas_call(
            y_kernel,
            name="y_terms",
            out_shape=local_shape((rows, BACK, LANES), bf16),
            scratch_shapes=[
                pltpu.VMEM((rows * 6 * y_own, LANES), f32),
                pltpu.VMEM((6, length_y, LANES), f32),
                pltpu.VMEM((2 * length_y, 3 * LANES), f32),
                pltpu.VMEM((length_y, 3 * LANES), f32),
                pltpu.VMEM((3, length_y, LANES), f32),
                pltpu.VMEM((rows * BACK, LANES), f32),
            ],
        )(near(lines), near(normal_pair))
        return exchange(terms, "rows")

    def along_z(keep, recv):
        pair = [part.reshape(chips, 1, 18, z_own, LANES) for part in (recv, keep)]
        lines = exchange(jnp.concatenate(pair, axis=1), "cols", axis_index_groups=alike)
        terms = pl.pallas_call(
            z_kernel,
            name="z_terms",
            out_shape=local_shape((chips, 2, 9, z_own, LANES), bf16),
            scratch_shapes=[
                pltpu.VMEM((2 * length_z, 9 * LANES), f32),
                pltpu.VMEM((length_z, 9 * LANES), f32),
            ],
        )(near(lines), near(span_pair))
        back = exchange(terms, "cols", axis_index_groups=alike)
        ordered = pl.pallas_call(
            order_kernel, name="order_z", out_shape=local_shape((rows, BACK, LANES), bf16)
        )(near(back))
        return ordered

    core = lax.axis_index("cols") % 2
    recv = lax.ppermute(pack(1, "pack_send", lambda x: x), "cols", partner)
    keep = pack(0, "pack_keep", near)
    base = x_terms()
    both = lax.cond(core == 0, along_y, along_z, keep, recv)
    other = lax.ppermute(both[rows // 2 :], "cols", partner)
    base = add(0, "add_own", base, both, local_shape)
    out = add(1, "add_other", base, other, jax.ShapeDtypeStruct)
    return out.transpose(0, 2, 1, 3)


def solution(mesh):
    placed = (P(None, "cols", "rows", None), P(None, "cols", "rows", None), P(), P(), P())
    return jax.shard_map(
        local, mesh=mesh, in_specs=placed, out_specs=P(None, "cols", "rows", None), check_vma=False
    )
```

```python
import functools

import jax
import jax.numpy as jnp
from jax import lax
from jax.experimental import pallas as pl
from jax.experimental.pallas import tpu as pltpu
from jax.sharding import PartitionSpec as P

viscosity = 0.5
section_step = 0.5
LANES = 128
BACK = 40


def fields(a_ref, u_ref, f, half):
    at = pl.ds(half * LANES, LANES)
    if f < 3:
        return a_ref[f, :, :, at]
    return u_ref[f - 3, :, :, at].astype(jnp.float32)


def pack_y(a_ref, u_ref, out_ref, stage):
    y_own, z_own = a_ref.shape[1:3]
    rows = 6 * y_own
    for f in range(6):
        for half in range(2):
            value = fields(a_ref, u_ref, f, half)
            for y in range(y_own):
                stage[pl.ds(half * rows + f * y_own + y, z_own, stride=2 * rows), :] = value[y]
    out_ref[...] = stage[...].reshape(2 * z_own, rows, LANES).astype(jnp.bfloat16)


def pack_z(a_ref, u_ref, out_ref):
    y_own, z_own = a_ref.shape[1:3]
    for f in range(6):
        for half in range(2):
            value = fields(a_ref, u_ref, f, half).astype(jnp.bfloat16)
            for y in range(y_own):
                row = ((y // 3 * 2 + half) * 18 + f * 3 + y % 3) * z_own
                out_ref[row // 72, pl.ds(row % 72, z_own), :] = value[y]


def pack_kernel(y_core, a_ref, u_ref, out_ref, stage):
    is_y = lax.axis_index("cols") % 2 == y_core

    @pl.when(is_y)
    def _():
        pack_y(a_ref, u_ref, out_ref, stage)

    @pl.when(jnp.logical_not(is_y))
    def _():
        pack_z(a_ref, u_ref, out_ref)


def x_kernel(a_ref, u_ref, px_ref, out_ref):
    comps, y_own, z_own, length = a_ref.shape
    rows = y_own * z_own
    px = px_ref[...]
    dims = (((1,), (1,)), ((), ()))
    adjoint = a_ref[...].reshape(comps * rows, length)
    a_b = adjoint.astype(jnp.bfloat16)
    u_f = u_ref[...].astype(jnp.float32).reshape(comps * rows, length)
    derivs = lax.dot_general(a_b, px, dims, preferred_element_type=jnp.float32)
    base_deriv = lax.dot_general(
        u_f.astype(jnp.bfloat16), px[:length], dims, preferred_element_type=jnp.float32
    )
    products = a_b.astype(jnp.float32) * base_deriv
    transfer = products[:rows] + products[rows : 2 * rows] + products[2 * rows :]
    u_dir = u_f[:rows]
    for c in range(comps):
        part = slice(c * rows, (c + 1) * rows)
        term = u_dir * derivs[part, :length] + viscosity * derivs[part, length:]
        if c == 0:
            term = term - transfer
        out_ref[c] = (adjoint[part] + section_step * term).reshape(y_own, z_own, length)


def z_kernel(rz_ref, pz_ref, oz_ref, derivs, base_derivs):
    chips, _, slabs, z_own = rz_ref.shape[:4]
    length = chips * 2 * z_own
    lines = [rz_ref[:, :, k].astype(jnp.float32).reshape(length, LANES) for k in range(slabs)]
    packed = [v.astype(jnp.bfloat16) for v in lines]
    pz = pz_ref[...]
    derivs[...] = jnp.dot(pz, jnp.concatenate(packed[:9], axis=1), preferred_element_type=jnp.float32)
    base_derivs[...] = jnp.dot(
        pz[:length], jnp.concatenate(packed[9:], axis=1), preferred_element_type=jnp.float32
    )
    for y in range(3):
        at = [pl.ds((3 * j + y) * LANES, LANES) for j in range(3)]
        u_dir = lines[9 + 3 * 2 + y]
        transfer = sum(lines[3 * j + y] * base_derivs[:, at[j]] for j in range(3))
        for c in range(3):
            term = u_dir * derivs[:length, at[c]] + viscosity * derivs[length:, at[c]]
            if c == 2:
                term = term - transfer
            oz_ref[:, :, 3 * c + y] = term.reshape(chips, 2, z_own, LANES).astype(jnp.bfloat16)


def y_kernel(ry_ref, py_ref, oy_ref, stage, lines, derivs, base_derivs, terms, back):
    peers, rows = ry_ref.shape[:2]
    y_own = rows // 6
    length = peers * y_own
    stage[...] = ry_ref[...].astype(jnp.float32).reshape(stage.shape)
    for f in range(6):
        for y in range(y_own):
            for g in range(peers // 8):
                lines[f, pl.ds(8 * g * y_own + y, 8, stride=y_own), :] = stage[
                    pl.ds(8 * g * rows + f * y_own + y, 8, stride=rows), :
                ]
    packed = [lines[f].astype(jnp.bfloat16) for f in range(6)]
    derivs[...] = jnp.dot(
        py_ref[...], jnp.concatenate(packed[:3], axis=1), preferred_element_type=jnp.float32
    )
    base_derivs[...] = jnp.dot(
        py_ref[pl.ds(0, length), :], jnp.concatenate(packed[3:], axis=1), preferred_element_type=jnp.float32
    )
    block = 48
    for b in range(length // block):
        at = pl.ds(b * block, block)
        lane = [pl.ds(j * LANES, LANES) for j in range(3)]
        u_dir = lines[4, at, :]
        transfer = sum(lines[j, at, :] * base_derivs[at, lane[j]] for j in range(3))
        for c in range(3):
            term = u_dir * derivs[at, lane[c]] + viscosity * derivs[pl.ds(length + b * block, block), lane[c]]
            if c == 1:
                term = term - transfer
            terms[c, at, :] = term
    for c in range(3):
        for y in range(y_own):
            for g in range(peers // 8):
                back[pl.ds(8 * g * BACK + c * y_own + y, 8, stride=BACK), :] = terms[
                    c, pl.ds(8 * g * y_own + y, 8, stride=y_own), :
                ]
    for p in range(peers):
        used = 3 * y_own
        back[pl.ds(p * BACK + used, BACK - used), :] = jnp.zeros((BACK - used, LANES), jnp.float32)
    oy_ref[...] = back[...].reshape(peers, BACK, LANES).astype(jnp.bfloat16)


def order_kernel(rz_ref, out_ref):
    pieces, _, slabs, z_own = rz_ref.shape[:4]
    for side in range(2):
        for p in range(pieces):
            for k in range(slabs):
                row = (p * slabs + k) * z_own
                out_ref[16 * side + row // BACK, pl.ds(row % BACK, z_own), :] = rz_ref[p, side, k]
        for row in range(pieces * slabs * z_own, 16 * BACK, z_own):
            out_ref[16 * side + row // BACK, pl.ds(row % BACK, z_own), :] = jnp.zeros((z_own, LANES), jnp.bfloat16)


def add_kernel(y_core, base_ref, part_ref, out_ref, stage):
    comps, y_own, z_own, _ = base_ref.shape
    is_y = lax.axis_index("cols") % 2 == y_core

    @pl.when(is_y)
    def _():
        stage[...] = part_ref[pl.ds(0, 16)].astype(jnp.float32).reshape(stage.shape)
        for c in range(comps):
            for y in range(y_own):
                for half in range(2):
                    at = pl.ds(half * LANES, LANES)
                    piece = stage[pl.ds(half * BACK + c * y_own + y, z_own, stride=2 * BACK), :]
                    out_ref[c, y, :, at] = base_ref[c, y, :, at] + section_step * piece

    @pl.when(jnp.logical_not(is_y))
    def _():
        for c in range(comps):
            for y in range(y_own):
                for half in range(2):
                    at = pl.ds(half * LANES, LANES)
                    row = ((y // 3 * 2 + half) * 9 + c * 3 + y % 3) * z_own
                    piece = part_ref[row // BACK, pl.ds(row % BACK, z_own), :].astype(jnp.float32)
                    out_ref[c, y, :, at] = base_ref[c, y, :, at] + section_step * piece


def local(adjoint, base_flow, stream_pair, normal_pair, span_pair):
    f32, bf16 = jnp.float32, jnp.bfloat16
    rows = lax.axis_size("rows")
    cols = lax.axis_size("cols")
    chips = cols // 2
    _, z_own, y_own, length_x = adjoint.shape
    length_y = rows * y_own
    length_z = cols * z_own
    a = adjoint.transpose(0, 2, 1, 3)
    u = base_flow.transpose(0, 2, 1, 3)
    local_shape = pltpu.VMEM
    near = functools.partial(pltpu.with_memory_space_constraint, memory_space=pltpu.VMEM)
    exchange = functools.partial(lax.all_to_all, split_axis=0, concat_axis=0, tiled=True)
    partner = [(i, i ^ 1) for i in range(cols)]
    alike = [list(range(core, cols, 2)) for core in range(2)]

    def pack(y_core, name, place):
        return pl.pallas_call(
            functools.partial(pack_kernel, y_core),
            name=name,
            out_shape=local_shape((2 * z_own, 6 * y_own, LANES), bf16),
            scratch_shapes=[pltpu.VMEM((2 * z_own * 6 * y_own, LANES), f32)],
        )(place(a), place(u))

    def x_terms():
        return pl.pallas_call(x_kernel, name="x_terms", out_shape=local_shape(a.shape, f32))(
            near(a), near(u), near(stream_pair)
        )

    def add(y_core, name, base, part, shape):
        return pl.pallas_call(
            functools.partial(add_kernel, y_core),
            name=name,
            out_shape=shape(a.shape, f32),
            scratch_shapes=[pltpu.VMEM((16 * BACK, LANES), f32)],
        )(near(base), near(part))

    def along_y(keep, recv):
        lines = exchange(jnp.concatenate([keep, recv], axis=0), "rows")
        terms = pl.pallas_call(
            y_kernel,
            name="y_terms",
            out_shape=local_shape((rows, BACK, LANES), bf16),
            scratch_shapes=[
                pltpu.VMEM((rows * 6 * y_own, LANES), f32),
                pltpu.VMEM((6, length_y, LANES), f32),
                pltpu.VMEM((2 * length_y, 3 * LANES), f32),
                pltpu.VMEM((length_y, 3 * LANES), f32),
                pltpu.VMEM((3, length_y, LANES), f32),
                pltpu.VMEM((rows * BACK, LANES), f32),
            ],
        )(near(lines), near(normal_pair))
        return exchange(terms, "rows")

    def along_z(keep, recv):
        pair = [part.reshape(chips, 1, 18, z_own, LANES) for part in (keep, recv)]
        lines = exchange(jnp.concatenate(pair, axis=1), "cols", axis_index_groups=alike)
        terms = pl.pallas_call(
            z_kernel,
            name="z_terms",
            out_shape=local_shape((chips, 2, 9, z_own, LANES), bf16),
            scratch_shapes=[
                pltpu.VMEM((2 * length_z, 9 * LANES), f32),
                pltpu.VMEM((length_z, 9 * LANES), f32),
            ],
        )(near(lines), near(span_pair))
        back = exchange(terms, "cols", axis_index_groups=alike)
        ordered = pl.pallas_call(
            order_kernel, name="order_z", out_shape=local_shape((rows, BACK, LANES), bf16)
        )(near(back))
        return ordered

    core = lax.axis_index("cols") % 2
    recv = lax.ppermute(pack(0, "pack_send", lambda x: x), "cols", partner)
    keep = pack(1, "pack_keep", near)
    base = x_terms()
    both = lax.cond(core == 1, along_y, along_z, keep, recv)
    other = lax.ppermute(both[rows // 2 :], "cols", partner)
    base = add(1, "add_own", base, both, local_shape)
    out = add(0, "add_other", base, other, jax.ShapeDtypeStruct)
    return out.transpose(0, 2, 1, 3)


def solution(mesh):
    placed = (P(None, "cols", "rows", None), P(None, "cols", "rows", None), P(), P(), P())
    return jax.shard_map(
        local, mesh=mesh, in_specs=placed, out_specs=P(None, "cols", "rows", None), check_vma=False
    )
```

```python
import functools

import jax
import jax.numpy as jnp
from jax import lax
from jax.experimental import pallas as pl
from jax.experimental.pallas import tpu as pltpu
from jax.sharding import PartitionSpec as P

viscosity = 0.5
section_step = 0.5
LANES = 128
BACK = 40


def pack_field(is_y, f, value, out_ref, stage, y_own, z_own):
    rows = 6 * y_own

    @pl.when(is_y)
    def _():
        for half in range(2):
            points = value(half)
            for y in range(y_own):
                stage[pl.ds(half * rows + f * y_own + y, z_own, stride=2 * rows), :] = points[y]

    @pl.when(jnp.logical_not(is_y))
    def _():
        for half in range(2):
            points = value(half).astype(jnp.bfloat16)
            for y in range(y_own):
                row = ((y // 3 * 2 + half) * 18 + f * 3 + y % 3) * z_own
                out_ref[row // 72, pl.ds(row % 72, z_own), :] = points[y]


def pack_fields(is_y, a_ref, u_ref, out_ref, stage, ready):
    for f in range(6):
        ready(f)
        ref, j = (a_ref, f) if f < 3 else (u_ref, f - 3)
        pack_field(
            is_y,
            f,
            lambda half: ref[j, :, :, pl.ds(half * LANES, LANES)].astype(jnp.float32),
            out_ref,
            stage,
            *ref.shape[1:3],
        )

    @pl.when(is_y)
    def _():
        out_ref[...] = stage[...].reshape(out_ref.shape).astype(jnp.bfloat16)


def pack_send_kernel(a_hbm, u_hbm, out_ref, a_ref, u_ref, stage, arrived):
    copies = [pltpu.make_async_copy(a_hbm.at[j], a_ref.at[j], arrived.at[j]) for j in range(3)]
    copies += [pltpu.make_async_copy(u_hbm.at[j], u_ref.at[j], arrived.at[3 + j]) for j in range(3)]
    for copy in copies:
        copy.start()
    is_y = lax.axis_index("cols") % 2 == 0
    pack_fields(is_y, a_ref, u_ref, out_ref, stage, lambda f: copies[f].wait())


def pack_keep_kernel(a_ref, u_ref, out_ref, stage):
    is_y = lax.axis_index("cols") % 2 == 1
    pack_fields(is_y, a_ref, u_ref, out_ref, stage, lambda f: None)


def x_kernel(a_ref, u_ref, px_ref, out_ref):
    comps, y_own, z_own, length = a_ref.shape
    rows = y_own * z_own
    px = px_ref[...]
    dims = (((1,), (1,)), ((), ()))
    adjoint = a_ref[...].reshape(comps * rows, length)
    a_b = adjoint.astype(jnp.bfloat16)
    u_f = u_ref[...].astype(jnp.float32).reshape(comps * rows, length)
    derivs = lax.dot_general(a_b, px, dims, preferred_element_type=jnp.float32)
    base_deriv = lax.dot_general(
        u_f.astype(jnp.bfloat16), px[:length], dims, preferred_element_type=jnp.float32
    )
    products = a_b.astype(jnp.float32) * base_deriv
    transfer = products[:rows] + products[rows : 2 * rows] + products[2 * rows :]
    u_dir = u_f[:rows]
    for c in range(comps):
        part = slice(c * rows, (c + 1) * rows)
        term = u_dir * derivs[part, :length] + viscosity * derivs[part, length:]
        if c == 0:
            term = term - transfer
        out_ref[c] = (adjoint[part] + section_step * term).reshape(y_own, z_own, length)


def z_kernel(rz_ref, pz_ref, oz_ref, derivs, base_derivs):
    chips, _, slabs, z_own = rz_ref.shape[:4]
    length = chips * 2 * z_own
    lines = [rz_ref[:, :, k].astype(jnp.float32).reshape(length, LANES) for k in range(slabs)]
    packed = [v.astype(jnp.bfloat16) for v in lines]
    pz = pz_ref[...]
    derivs[...] = jnp.dot(pz, jnp.concatenate(packed[:9], axis=1), preferred_element_type=jnp.float32)
    base_derivs[...] = jnp.dot(
        pz[:length], jnp.concatenate(packed[9:], axis=1), preferred_element_type=jnp.float32
    )
    for y in range(3):
        at = [pl.ds((3 * j + y) * LANES, LANES) for j in range(3)]
        u_dir = lines[9 + 3 * 2 + y]
        transfer = sum(lines[3 * j + y] * base_derivs[:, at[j]] for j in range(3))
        for c in range(3):
            term = u_dir * derivs[:length, at[c]] + viscosity * derivs[length:, at[c]]
            if c == 2:
                term = term - transfer
            oz_ref[:, :, 3 * c + y] = term.reshape(chips, 2, z_own, LANES).astype(jnp.bfloat16)


def y_kernel(ry_ref, py_ref, oy_ref, stage, lines, derivs, base_derivs, terms, back):
    peers, rows = ry_ref.shape[:2]
    y_own = rows // 6
    length = peers * y_own
    stage[...] = ry_ref[...].astype(jnp.float32).reshape(stage.shape)
    for f in range(6):
        for y in range(y_own):
            for g in range(peers // 8):
                lines[f, pl.ds(8 * g * y_own + y, 8, stride=y_own), :] = stage[
                    pl.ds(8 * g * rows + f * y_own + y, 8, stride=rows), :
                ]
    packed = [lines[f].astype(jnp.bfloat16) for f in range(6)]
    derivs[...] = jnp.dot(
        py_ref[...], jnp.concatenate(packed[:3], axis=1), preferred_element_type=jnp.float32
    )
    base_derivs[...] = jnp.dot(
        py_ref[pl.ds(0, length), :], jnp.concatenate(packed[3:], axis=1), preferred_element_type=jnp.float32
    )
    block = 48
    for b in range(length // block):
        at = pl.ds(b * block, block)
        lane = [pl.ds(j * LANES, LANES) for j in range(3)]
        u_dir = lines[4, at, :]
        transfer = sum(lines[j, at, :] * base_derivs[at, lane[j]] for j in range(3))
        for c in range(3):
            term = u_dir * derivs[at, lane[c]] + viscosity * derivs[pl.ds(length + b * block, block), lane[c]]
            if c == 1:
                term = term - transfer
            terms[c, at, :] = term
    for c in range(3):
        for y in range(y_own):
            for g in range(peers // 8):
                back[pl.ds(8 * g * BACK + c * y_own + y, 8, stride=BACK), :] = terms[
                    c, pl.ds(8 * g * y_own + y, 8, stride=y_own), :
                ]
    for p in range(peers):
        used = 3 * y_own
        back[pl.ds(p * BACK + used, BACK - used), :] = jnp.zeros((BACK - used, LANES), jnp.float32)
    oy_ref[...] = back[...].reshape(peers, BACK, LANES).astype(jnp.bfloat16)


def order_kernel(rz_ref, out_ref):
    pieces, _, slabs, z_own = rz_ref.shape[:4]
    for side in range(2):
        for p in range(pieces):
            for k in range(slabs):
                row = (p * slabs + k) * z_own
                out_ref[16 * side + row // BACK, pl.ds(row % BACK, z_own), :] = rz_ref[p, side, k]
        for row in range(pieces * slabs * z_own, 16 * BACK, z_own):
            out_ref[16 * side + row // BACK, pl.ds(row % BACK, z_own), :] = jnp.zeros((z_own, LANES), jnp.bfloat16)


def add_parts(is_y, base_ref, part_ref, out_ref, stage, done):
    comps, y_own, z_own, _ = base_ref.shape

    @pl.when(is_y)
    def _():
        stage[...] = part_ref[pl.ds(0, 16)].astype(jnp.float32).reshape(stage.shape)

    for c in range(comps):

        @pl.when(is_y)
        def _():
            for y in range(y_own):
                for half in range(2):
                    at = pl.ds(half * LANES, LANES)
                    piece = stage[pl.ds(half * BACK + c * y_own + y, z_own, stride=2 * BACK), :]
                    out_ref[c, y, :, at] = base_ref[c, y, :, at] + section_step * piece

        @pl.when(jnp.logical_not(is_y))
        def _():
            for y in range(y_own):
                for half in range(2):
                    at = pl.ds(half * LANES, LANES)
                    row = ((y // 3 * 2 + half) * 9 + c * 3 + y % 3) * z_own
                    piece = part_ref[row // BACK, pl.ds(row % BACK, z_own), :].astype(jnp.float32)
                    out_ref[c, y, :, at] = base_ref[c, y, :, at] + section_step * piece

        done(c)


def add_own_kernel(base_ref, part_ref, out_ref, stage):
    is_y = lax.axis_index("cols") % 2 == 1
    add_parts(is_y, base_ref, part_ref, out_ref, stage, lambda c: None)


def add_other_kernel(base_ref, part_ref, out_hbm, stage, total, left):
    is_y = lax.axis_index("cols") % 2 == 0
    copies = [pltpu.make_async_copy(total.at[c], out_hbm.at[c], left.at[c]) for c in range(3)]
    add_parts(is_y, base_ref, part_ref, total, stage, lambda c: copies[c].start())
    for copy in copies:
        copy.wait()


def local(adjoint, base_flow, stream_pair, normal_pair, span_pair):
    f32, bf16 = jnp.float32, jnp.bfloat16
    rows = lax.axis_size("rows")
    cols = lax.axis_size("cols")
    chips = cols // 2
    _, z_own, y_own, length_x = adjoint.shape
    length_y = rows * y_own
    length_z = cols * z_own
    a = adjoint.transpose(0, 2, 1, 3)
    u = base_flow.transpose(0, 2, 1, 3)
    local_shape = pltpu.VMEM
    near = functools.partial(pltpu.with_memory_space_constraint, memory_space=pltpu.VMEM)
    exchange = functools.partial(lax.all_to_all, split_axis=0, concat_axis=0, tiled=True)
    partner = [(i, i ^ 1) for i in range(cols)]
    alike = [list(range(core, cols, 2)) for core in range(2)]

    def along_y(keep, recv):
        lines = exchange(jnp.concatenate([keep, recv], axis=0), "rows")
        terms = pl.pallas_call(
            y_kernel,
            name="y_terms",
            out_shape=local_shape((rows, BACK, LANES), bf16),
            scratch_shapes=[
                pltpu.VMEM((rows * 6 * y_own, LANES), f32),
                pltpu.VMEM((6, length_y, LANES), f32),
                pltpu.VMEM((2 * length_y, 3 * LANES), f32),
                pltpu.VMEM((length_y, 3 * LANES), f32),
                pltpu.VMEM((3, length_y, LANES), f32),
                pltpu.VMEM((rows * BACK, LANES), f32),
            ],
        )(near(lines), near(normal_pair))
        return exchange(terms, "rows")

    def along_z(keep, recv):
        pair = [part.reshape(chips, 1, 18, z_own, LANES) for part in (keep, recv)]
        lines = exchange(jnp.concatenate(pair, axis=1), "cols", axis_index_groups=alike)
        terms = pl.pallas_call(
            z_kernel,
            name="z_terms",
            out_shape=local_shape((chips, 2, 9, z_own, LANES), bf16),
            scratch_shapes=[
                pltpu.VMEM((2 * length_z, 9 * LANES), f32),
                pltpu.VMEM((length_z, 9 * LANES), f32),
            ],
        )(near(lines), near(span_pair))
        back = exchange(terms, "cols", axis_index_groups=alike)
        ordered = pl.pallas_call(
            order_kernel, name="order_z", out_shape=local_shape((rows, BACK, LANES), bf16)
        )(near(back))
        return ordered

    packed = (2 * z_own, 6 * y_own, LANES)
    pack_stage = pltpu.VMEM((2 * z_own * 6 * y_own, LANES), f32)
    send, a, u = pl.pallas_call(
        pack_send_kernel,
        name="pack_send",
        in_specs=[pl.BlockSpec(memory_space=pl.ANY)] * 2,
        out_shape=(local_shape(packed, bf16), local_shape(a.shape, f32), local_shape(u.shape, bf16)),
        scratch_shapes=[pack_stage, pltpu.SemaphoreType.DMA((6,))],
    )(a, u)
    send, normal_pair = lax.optimization_barrier((send, normal_pair))
    recv = lax.ppermute(send, "cols", partner)
    keep = pl.pallas_call(
        pack_keep_kernel, name="pack_keep", out_shape=local_shape(packed, bf16), scratch_shapes=[pack_stage]
    )(near(a), near(u))
    base = pl.pallas_call(x_kernel, name="x_terms", out_shape=local_shape(a.shape, f32))(
        near(a), near(u), near(stream_pair)
    )
    both = lax.cond(lax.axis_index("cols") % 2 == 1, along_y, along_z, keep, recv)
    other = lax.ppermute(both[rows // 2 :], "cols", partner)
    add_stage = pltpu.VMEM((16 * BACK, LANES), f32)
    base = pl.pallas_call(
        add_own_kernel, name="add_own", out_shape=local_shape(a.shape, f32), scratch_shapes=[add_stage]
    )(near(base), near(both))
    out = pl.pallas_call(
        add_other_kernel,
        name="add_other",
        out_shape=jax.ShapeDtypeStruct(a.shape, f32),
        out_specs=pl.BlockSpec(memory_space=pl.ANY),
        scratch_shapes=[add_stage, pltpu.VMEM(a.shape, f32), pltpu.SemaphoreType.DMA((3,))],
    )(near(base), near(other))
    return out.transpose(0, 2, 1, 3)


def solution(mesh):
    placed = (P(None, "cols", "rows", None), P(None, "cols", "rows", None), P(), P(), P())
    return jax.shard_map(
        local, mesh=mesh, in_specs=placed, out_specs=P(None, "cols", "rows", None), check_vma=False
    )
```

```python
import functools

import jax
import jax.numpy as jnp
from jax import lax
from jax.experimental import pallas as pl
from jax.experimental.pallas import tpu as pltpu
from jax.sharding import PartitionSpec as P

viscosity = 0.5
section_step = 0.5
LANES = 128
BACK = 40


def pack_field(is_y, f, value, out_ref, stage, y_own, z_own):
    rows = 6 * y_own

    @pl.when(is_y)
    def _():
        for half in range(2):
            points = value(half)
            for y in range(y_own):
                stage[pl.ds(half * rows + f * y_own + y, z_own, stride=2 * rows), :] = points[y]

    @pl.when(jnp.logical_not(is_y))
    def _():
        for half in range(2):
            points = value(half).astype(jnp.bfloat16)
            for y in range(y_own):
                row = ((y // 3 * 2 + half) * 18 + f * 3 + y % 3) * z_own
                out_ref[row // 72, pl.ds(row % 72, z_own), :] = points[y]


def pack_fields(is_y, a_ref, u_ref, out_ref, stage, ready):
    for f in range(6):
        ready(f)
        ref, j = (a_ref, f) if f < 3 else (u_ref, f - 3)
        pack_field(
            is_y,
            f,
            lambda half: ref[j, :, :, pl.ds(half * LANES, LANES)].astype(jnp.float32),
            out_ref,
            stage,
            *ref.shape[1:3],
        )

    @pl.when(is_y)
    def _():
        out_ref[...] = stage[...].reshape(out_ref.shape).astype(jnp.bfloat16)


def pack_send_kernel(a_hbm, u_hbm, out_ref, a_ref, u_ref, stage, arrived):
    copies = [pltpu.make_async_copy(a_hbm.at[j], a_ref.at[j], arrived.at[j]) for j in range(3)]
    copies += [pltpu.make_async_copy(u_hbm.at[j], u_ref.at[j], arrived.at[3 + j]) for j in range(3)]
    for copy in copies:
        copy.start()
    is_y = lax.axis_index("cols") % 2 == 0
    pack_fields(is_y, a_ref, u_ref, out_ref, stage, lambda f: copies[f].wait())


def pack_keep_kernel(a_ref, u_ref, out_ref, stage):
    is_y = lax.axis_index("cols") % 2 == 1
    pack_fields(is_y, a_ref, u_ref, out_ref, stage, lambda f: None)


def x_kernel(a_ref, u_ref, px_ref, out_ref):
    comps, y_own, z_own, length = a_ref.shape
    rows = y_own * z_own
    px = px_ref[...]
    dims = (((1,), (1,)), ((), ()))
    adjoint = a_ref[...].reshape(comps * rows, length)
    a_b = adjoint.astype(jnp.bfloat16)
    u_f = u_ref[...].astype(jnp.float32).reshape(comps * rows, length)
    derivs = lax.dot_general(a_b, px, dims, preferred_element_type=jnp.float32)
    base_deriv = lax.dot_general(
        u_f.astype(jnp.bfloat16), px[:length], dims, preferred_element_type=jnp.float32
    )
    products = a_b.astype(jnp.float32) * base_deriv
    transfer = products[:rows] + products[rows : 2 * rows] + products[2 * rows :]
    u_dir = u_f[:rows]
    for c in range(comps):
        part = slice(c * rows, (c + 1) * rows)
        term = u_dir * derivs[part, :length] + viscosity * derivs[part, length:]
        if c == 0:
            term = term - transfer
        out_ref[c] = (adjoint[part] + section_step * term).reshape(y_own, z_own, length)


def z_kernel(rz_ref, pz_ref, oz_ref, derivs, base_derivs):
    chips, _, slabs, z_own = rz_ref.shape[:4]
    length = chips * 2 * z_own
    lines = [rz_ref[:, :, k].astype(jnp.float32).reshape(length, LANES) for k in range(slabs)]
    packed = [v.astype(jnp.bfloat16) for v in lines]
    pz = pz_ref[...]
    derivs[...] = jnp.dot(pz, jnp.concatenate(packed[:9], axis=1), preferred_element_type=jnp.float32)
    base_derivs[...] = jnp.dot(
        pz[:length], jnp.concatenate(packed[9:], axis=1), preferred_element_type=jnp.float32
    )
    for y in range(3):
        at = [pl.ds((3 * j + y) * LANES, LANES) for j in range(3)]
        u_dir = lines[9 + 3 * 2 + y]
        transfer = sum(lines[3 * j + y] * base_derivs[:, at[j]] for j in range(3))
        for c in range(3):
            term = u_dir * derivs[:length, at[c]] + viscosity * derivs[length:, at[c]]
            if c == 2:
                term = term - transfer
            oz_ref[:, :, 3 * c + y] = term.reshape(chips, 2, z_own, LANES).astype(jnp.bfloat16)


def permute_kernel(py_ref, out_ref):
    length = py_ref.shape[1]
    row = lax.broadcasted_iota(jnp.int32, (length, length), 0)
    eight = row >> 3
    group = (eight * 43) >> 9
    source = group * 96 + (row & 7) * 12 + (eight - group * 12)
    column = lax.broadcasted_iota(jnp.int32, (length, length), 1)
    pick = jnp.where(source == column, 1.0, 0.0).astype(jnp.bfloat16)
    dims = (((1,), (1,)), ((), ()))
    for h in range(2):
        at = pl.ds(h * length, length)
        rows = jnp.dot(pick, py_ref[at, :], preferred_element_type=jnp.float32).astype(jnp.bfloat16)
        both = lax.dot_general(rows, pick, dims, preferred_element_type=jnp.float32)
        out_ref[at, :] = both.astype(jnp.bfloat16)


def y_kernel(ry_ref, py_ref, oy_ref, stage, derivs, base_derivs, back):
    peers, rows = ry_ref.shape[:2]
    y_own = rows // 6
    length = peers * y_own
    stage[...] = ry_ref[...].astype(jnp.float32).reshape(stage.shape)
    order = [(g, w) for g in range(peers // 8) for w in range(y_own)]

    def points(f, g, w):
        return stage[pl.ds(8 * g * rows + f * y_own + w, 8, stride=rows), :]

    packed = [jnp.concatenate([points(f, *at) for at in order], axis=0).astype(jnp.bfloat16) for f in range(6)]
    derivs[...] = jnp.dot(
        py_ref[...], jnp.concatenate(packed[:3], axis=1), preferred_element_type=jnp.float32
    )
    base_derivs[...] = jnp.dot(
        py_ref[pl.ds(0, length), :], jnp.concatenate(packed[3:], axis=1), preferred_element_type=jnp.float32
    )
    lane = [pl.ds(j * LANES, LANES) for j in range(3)]
    for i, (g, w) in enumerate(order):
        at, second = pl.ds(8 * i, 8), pl.ds(length + 8 * i, 8)
        u_dir = points(4, g, w)
        transfer = sum(points(j, g, w) * base_derivs[at, lane[j]] for j in range(3))
        for c in range(3):
            term = u_dir * derivs[at, lane[c]] + viscosity * derivs[second, lane[c]]
            if c == 1:
                term = term - transfer
            back[pl.ds(8 * g * BACK + c * y_own + w, 8, stride=BACK), :] = term
    for p in range(peers):
        used = 3 * y_own
        back[pl.ds(p * BACK + used, BACK - used), :] = jnp.zeros((BACK - used, LANES), jnp.float32)
    oy_ref[...] = back[...].reshape(peers, BACK, LANES).astype(jnp.bfloat16)


def order_kernel(rz_ref, out_ref):
    pieces, _, slabs, z_own = rz_ref.shape[:4]
    for side in range(2):
        for p in range(pieces):
            for k in range(slabs):
                row = (p * slabs + k) * z_own
                out_ref[16 * side + row // BACK, pl.ds(row % BACK, z_own), :] = rz_ref[p, side, k]
        for row in range(pieces * slabs * z_own, 16 * BACK, z_own):
            out_ref[16 * side + row // BACK, pl.ds(row % BACK, z_own), :] = jnp.zeros((z_own, LANES), jnp.bfloat16)


def add_parts(is_y, base_ref, part_ref, out_ref, stage, done):
    comps, y_own, z_own, _ = base_ref.shape

    @pl.when(is_y)
    def _():
        stage[...] = part_ref[pl.ds(0, 16)].astype(jnp.float32).reshape(stage.shape)

    for c in range(comps):

        @pl.when(is_y)
        def _():
            for y in range(y_own):
                for half in range(2):
                    at = pl.ds(half * LANES, LANES)
                    piece = stage[pl.ds(half * BACK + c * y_own + y, z_own, stride=2 * BACK), :]
                    out_ref[c, y, :, at] = base_ref[c, y, :, at] + section_step * piece

        @pl.when(jnp.logical_not(is_y))
        def _():
            for y in range(y_own):
                for half in range(2):
                    at = pl.ds(half * LANES, LANES)
                    row = ((y // 3 * 2 + half) * 9 + c * 3 + y % 3) * z_own
                    piece = part_ref[row // BACK, pl.ds(row % BACK, z_own), :].astype(jnp.float32)
                    out_ref[c, y, :, at] = base_ref[c, y, :, at] + section_step * piece

        done(c)


def add_own_kernel(base_ref, part_ref, out_ref, stage):
    is_y = lax.axis_index("cols") % 2 == 1
    add_parts(is_y, base_ref, part_ref, out_ref, stage, lambda c: None)


def add_other_kernel(base_ref, part_ref, out_hbm, stage, total, left):
    is_y = lax.axis_index("cols") % 2 == 0
    copies = [pltpu.make_async_copy(total.at[c], out_hbm.at[c], left.at[c]) for c in range(3)]
    add_parts(is_y, base_ref, part_ref, total, stage, lambda c: copies[c].start())
    for copy in copies:
        copy.wait()


def local(adjoint, base_flow, stream_pair, normal_pair, span_pair):
    f32, bf16 = jnp.float32, jnp.bfloat16
    rows = lax.axis_size("rows")
    cols = lax.axis_size("cols")
    chips = cols // 2
    _, z_own, y_own, length_x = adjoint.shape
    length_y = rows * y_own
    length_z = cols * z_own
    a = adjoint.transpose(0, 2, 1, 3)
    u = base_flow.transpose(0, 2, 1, 3)
    local_shape = pltpu.VMEM
    near = functools.partial(pltpu.with_memory_space_constraint, memory_space=pltpu.VMEM)
    exchange = functools.partial(lax.all_to_all, split_axis=0, concat_axis=0, tiled=True)
    partner = [(i, i ^ 1) for i in range(cols)]
    alike = [list(range(core, cols, 2)) for core in range(2)]

    def along_y(keep, recv):
        lines = exchange(jnp.concatenate([keep, recv], axis=0), "rows")
        terms = pl.pallas_call(
            y_kernel,
            name="y_terms",
            out_shape=local_shape((rows, BACK, LANES), bf16),
            scratch_shapes=[
                pltpu.VMEM((rows * 6 * y_own, LANES), f32),
                pltpu.VMEM((2 * length_y, 3 * LANES), f32),
                pltpu.VMEM((length_y, 3 * LANES), f32),
                pltpu.VMEM((rows * BACK, LANES), f32),
            ],
        )(near(lines), near(normal_pair))
        return exchange(terms, "rows")

    def along_z(keep, recv):
        pair = [part.reshape(chips, 1, 18, z_own, LANES) for part in (keep, recv)]
        lines = exchange(jnp.concatenate(pair, axis=1), "cols", axis_index_groups=alike)
        terms = pl.pallas_call(
            z_kernel,
            name="z_terms",
            out_shape=local_shape((chips, 2, 9, z_own, LANES), bf16),
            scratch_shapes=[
                pltpu.VMEM((2 * length_z, 9 * LANES), f32),
                pltpu.VMEM((length_z, 9 * LANES), f32),
            ],
        )(near(lines), near(span_pair))
        back = exchange(terms, "cols", axis_index_groups=alike)
        ordered = pl.pallas_call(
            order_kernel, name="order_z", out_shape=local_shape((rows, BACK, LANES), bf16)
        )(near(back))
        return ordered

    packed = (2 * z_own, 6 * y_own, LANES)
    pack_stage = pltpu.VMEM((2 * z_own * 6 * y_own, LANES), f32)
    send, a, u = pl.pallas_call(
        pack_send_kernel,
        name="pack_send",
        in_specs=[pl.BlockSpec(memory_space=pl.ANY)] * 2,
        out_shape=(local_shape(packed, bf16), local_shape(a.shape, f32), local_shape(u.shape, bf16)),
        scratch_shapes=[pack_stage, pltpu.SemaphoreType.DMA((6,))],
    )(a, u)
    recv = lax.ppermute(send, "cols", partner)
    keep = pl.pallas_call(
        pack_keep_kernel, name="pack_keep", out_shape=local_shape(packed, bf16), scratch_shapes=[pack_stage]
    )(near(a), near(u))
    normal_pair = pl.pallas_call(
        permute_kernel, name="permute_y", out_shape=local_shape(normal_pair.shape, bf16)
    )(near(normal_pair))
    base = pl.pallas_call(x_kernel, name="x_terms", out_shape=local_shape(a.shape, f32))(
        near(a), near(u), near(stream_pair)
    )
    both = lax.cond(lax.axis_index("cols") % 2 == 1, along_y, along_z, keep, recv)
    other = lax.ppermute(both[rows // 2 :], "cols", partner)
    add_stage = pltpu.VMEM((16 * BACK, LANES), f32)
    base = pl.pallas_call(
        add_own_kernel, name="add_own", out_shape=local_shape(a.shape, f32), scratch_shapes=[add_stage]
    )(near(base), near(both))
    out = pl.pallas_call(
        add_other_kernel,
        name="add_other",
        out_shape=jax.ShapeDtypeStruct(a.shape, f32),
        out_specs=pl.BlockSpec(memory_space=pl.ANY),
        scratch_shapes=[add_stage, pltpu.VMEM(a.shape, f32), pltpu.SemaphoreType.DMA((3,))],
    )(near(base), near(other))
    return out.transpose(0, 2, 1, 3)


def solution(mesh):
    placed = (P(None, "cols", "rows", None), P(None, "cols", "rows", None), P(), P(), P())
    return jax.shard_map(
        local, mesh=mesh, in_specs=placed, out_specs=P(None, "cols", "rows", None), check_vma=False
    )
```

```python
import functools

import jax
import jax.numpy as jnp
from jax import lax
from jax.experimental import pallas as pl
from jax.experimental.pallas import tpu as pltpu
from jax.sharding import PartitionSpec as P

viscosity = 0.5
section_step = 0.5
LANES = 128
BACK = 40


def pack_field(is_y, f, value, out_ref, stage, y_own, z_own):
    rows = 6 * y_own

    @pl.when(is_y)
    def _():
        for half in range(2):
            points = value(half)
            for y in range(y_own):
                stage[pl.ds(half * rows + f * y_own + y, z_own, stride=2 * rows), :] = points[y]

    @pl.when(jnp.logical_not(is_y))
    def _():
        for half in range(2):
            points = value(half).astype(jnp.bfloat16)
            for y in range(y_own):
                row = ((y // 3 * 2 + half) * 18 + f * 3 + y % 3) * z_own
                out_ref[row // 72, pl.ds(row % 72, z_own), :] = points[y]


def pack_fields(is_y, a_ref, u_ref, out_ref, stage, ready):
    for f in range(6):
        ready(f)
        ref, j = (a_ref, f) if f < 3 else (u_ref, f - 3)
        pack_field(
            is_y,
            f,
            lambda half: ref[j, :, :, pl.ds(half * LANES, LANES)].astype(jnp.float32),
            out_ref,
            stage,
            *ref.shape[1:3],
        )

    @pl.when(is_y)
    def _():
        out_ref[...] = stage[...].reshape(out_ref.shape).astype(jnp.bfloat16)


def pack_send_kernel(a_hbm, u_hbm, out_ref, a_ref, u_ref, stage, arrived):
    copies = [pltpu.make_async_copy(a_hbm.at[j], a_ref.at[j], arrived.at[j]) for j in range(3)]
    copies += [pltpu.make_async_copy(u_hbm.at[j], u_ref.at[j], arrived.at[3 + j]) for j in range(3)]
    for copy in copies:
        copy.start()
    is_y = lax.axis_index("cols") % 2 == 0
    pack_fields(is_y, a_ref, u_ref, out_ref, stage, lambda f: copies[f].wait())


def pack_keep_kernel(a_ref, u_ref, out_ref, stage):
    is_y = lax.axis_index("cols") % 2 == 1
    pack_fields(is_y, a_ref, u_ref, out_ref, stage, lambda f: None)


def x_kernel(a_ref, u_ref, px_ref, out_ref):
    comps, y_own, z_own, length = a_ref.shape
    rows = y_own * z_own
    px = px_ref[...]
    dims = (((1,), (1,)), ((), ()))
    adjoint = a_ref[...].reshape(comps * rows, length)
    a_b = adjoint.astype(jnp.bfloat16)
    u_f = u_ref[...].astype(jnp.float32).reshape(comps * rows, length)
    derivs = lax.dot_general(a_b, px, dims, preferred_element_type=jnp.float32)
    base_deriv = lax.dot_general(
        u_f.astype(jnp.bfloat16), px[:length], dims, preferred_element_type=jnp.float32
    )
    products = a_b.astype(jnp.float32) * base_deriv
    transfer = products[:rows] + products[rows : 2 * rows] + products[2 * rows :]
    u_dir = u_f[:rows]
    for c in range(comps):
        part = slice(c * rows, (c + 1) * rows)
        term = u_dir * derivs[part, :length] + viscosity * derivs[part, length:]
        if c == 0:
            term = term - transfer
        out_ref[c] = (adjoint[part] + section_step * term).reshape(y_own, z_own, length)


def z_kernel(rz_ref, pz_ref, oz_ref, derivs, base_derivs):
    chips, _, slabs, z_own = rz_ref.shape[:4]
    length = chips * 2 * z_own
    lines = [rz_ref[:, :, k].astype(jnp.float32).reshape(length, LANES) for k in range(slabs)]
    packed = [v.astype(jnp.bfloat16) for v in lines]
    pz = pz_ref[...]
    derivs[...] = jnp.dot(pz, jnp.concatenate(packed[:9], axis=1), preferred_element_type=jnp.float32)
    base_derivs[...] = jnp.dot(
        pz[:length], jnp.concatenate(packed[9:], axis=1), preferred_element_type=jnp.float32
    )
    for y in range(3):
        at = [pl.ds((3 * j + y) * LANES, LANES) for j in range(3)]
        u_dir = lines[9 + 3 * 2 + y]
        transfer = sum(lines[3 * j + y] * base_derivs[:, at[j]] for j in range(3))
        for c in range(3):
            term = u_dir * derivs[:length, at[c]] + viscosity * derivs[length:, at[c]]
            if c == 2:
                term = term - transfer
            oz_ref[:, :, 3 * c + y] = term.reshape(chips, 2, z_own, LANES).astype(jnp.bfloat16)


def y_kernel(ry_ref, py_ref, oy_ref, lines, derivs, base_derivs, terms):
    peers, rows = ry_ref.shape[:2]
    y_own = rows // 6
    length = peers * y_own
    for f in range(6):
        for p in range(peers):
            lines[f, pl.ds(p * y_own, y_own), :] = ry_ref[p, pl.ds(f * y_own, y_own), :].astype(jnp.float32)
    packed = [lines[f].astype(jnp.bfloat16) for f in range(6)]
    derivs[...] = jnp.dot(
        py_ref[...], jnp.concatenate(packed[:3], axis=1), preferred_element_type=jnp.float32
    )
    base_derivs[...] = jnp.dot(
        py_ref[pl.ds(0, length), :], jnp.concatenate(packed[3:], axis=1), preferred_element_type=jnp.float32
    )
    block = 48
    for b in range(length // block):
        at = pl.ds(b * block, block)
        lane = [pl.ds(j * LANES, LANES) for j in range(3)]
        u_dir = lines[4, at, :]
        transfer = sum(lines[j, at, :] * base_derivs[at, lane[j]] for j in range(3))
        for c in range(3):
            term = u_dir * derivs[at, lane[c]] + viscosity * derivs[pl.ds(length + b * block, block), lane[c]]
            if c == 1:
                term = term - transfer
            terms[c, at, :] = term
    for p in range(peers):
        parts = [terms[c, pl.ds(p * y_own, y_own), :] for c in range(3)]
        parts.append(jnp.zeros((BACK - 3 * y_own, LANES), jnp.float32))
        oy_ref[p] = jnp.concatenate(parts, axis=0).astype(jnp.bfloat16)


def order_kernel(rz_ref, out_ref):
    pieces, _, slabs, z_own = rz_ref.shape[:4]
    for side in range(2):
        for p in range(pieces):
            for k in range(slabs):
                row = (p * slabs + k) * z_own
                out_ref[16 * side + row // BACK, pl.ds(row % BACK, z_own), :] = rz_ref[p, side, k]
        for row in range(pieces * slabs * z_own, 16 * BACK, z_own):
            out_ref[16 * side + row // BACK, pl.ds(row % BACK, z_own), :] = jnp.zeros((z_own, LANES), jnp.bfloat16)


def add_parts(is_y, base_ref, part_ref, out_ref, stage, done):
    comps, y_own, z_own, _ = base_ref.shape

    @pl.when(is_y)
    def _():
        stage[...] = part_ref[pl.ds(0, 16)].astype(jnp.float32).reshape(stage.shape)

    for c in range(comps):

        @pl.when(is_y)
        def _():
            for y in range(y_own):
                for half in range(2):
                    at = pl.ds(half * LANES, LANES)
                    piece = stage[pl.ds(half * BACK + c * y_own + y, z_own, stride=2 * BACK), :]
                    out_ref[c, y, :, at] = base_ref[c, y, :, at] + section_step * piece

        @pl.when(jnp.logical_not(is_y))
        def _():
            for y in range(y_own):
                for half in range(2):
                    at = pl.ds(half * LANES, LANES)
                    row = ((y // 3 * 2 + half) * 9 + c * 3 + y % 3) * z_own
                    piece = part_ref[row // BACK, pl.ds(row % BACK, z_own), :].astype(jnp.float32)
                    out_ref[c, y, :, at] = base_ref[c, y, :, at] + section_step * piece

        done(c)


def add_own_kernel(base_ref, part_ref, out_ref, stage):
    is_y = lax.axis_index("cols") % 2 == 1
    add_parts(is_y, base_ref, part_ref, out_ref, stage, lambda c: None)


def add_other_kernel(base_ref, part_ref, out_hbm, stage, total, left):
    is_y = lax.axis_index("cols") % 2 == 0
    copies = [pltpu.make_async_copy(total.at[c], out_hbm.at[c], left.at[c]) for c in range(3)]
    add_parts(is_y, base_ref, part_ref, total, stage, lambda c: copies[c].start())
    for copy in copies:
        copy.wait()


def local(adjoint, base_flow, stream_pair, normal_pair, span_pair):
    f32, bf16 = jnp.float32, jnp.bfloat16
    rows = lax.axis_size("rows")
    cols = lax.axis_size("cols")
    chips = cols // 2
    _, z_own, y_own, length_x = adjoint.shape
    length_y = rows * y_own
    length_z = cols * z_own
    a = adjoint.transpose(0, 2, 1, 3)
    u = base_flow.transpose(0, 2, 1, 3)
    local_shape = pltpu.VMEM
    near = functools.partial(pltpu.with_memory_space_constraint, memory_space=pltpu.VMEM)
    exchange = functools.partial(lax.all_to_all, split_axis=0, concat_axis=0, tiled=True)
    partner = [(i, i ^ 1) for i in range(cols)]
    alike = [list(range(core, cols, 2)) for core in range(2)]

    def along_y(keep, recv):
        lines = exchange(jnp.concatenate([keep, recv], axis=0), "rows")
        terms = pl.pallas_call(
            y_kernel,
            name="y_terms",
            out_shape=local_shape((rows, BACK, LANES), bf16),
            scratch_shapes=[
                pltpu.VMEM((6, length_y, LANES), f32),
                pltpu.VMEM((2 * length_y, 3 * LANES), f32),
                pltpu.VMEM((length_y, 3 * LANES), f32),
                pltpu.VMEM((3, length_y, LANES), f32),
            ],
        )(near(lines), near(normal_pair))
        return exchange(terms, "rows")

    def along_z(keep, recv):
        pair = [part.reshape(chips, 1, 18, z_own, LANES) for part in (keep, recv)]
        lines = exchange(jnp.concatenate(pair, axis=1), "cols", axis_index_groups=alike)
        terms = pl.pallas_call(
            z_kernel,
            name="z_terms",
            out_shape=local_shape((chips, 2, 9, z_own, LANES), bf16),
            scratch_shapes=[
                pltpu.VMEM((2 * length_z, 9 * LANES), f32),
                pltpu.VMEM((length_z, 9 * LANES), f32),
            ],
        )(near(lines), near(span_pair))
        back = exchange(terms, "cols", axis_index_groups=alike)
        ordered = pl.pallas_call(
            order_kernel, name="order_z", out_shape=local_shape((rows, BACK, LANES), bf16)
        )(near(back))
        return ordered

    packed = (2 * z_own, 6 * y_own, LANES)
    pack_stage = pltpu.VMEM((2 * z_own * 6 * y_own, LANES), f32)
    send, a, u = pl.pallas_call(
        pack_send_kernel,
        name="pack_send",
        in_specs=[pl.BlockSpec(memory_space=pl.ANY)] * 2,
        out_shape=(local_shape(packed, bf16), local_shape(a.shape, f32), local_shape(u.shape, bf16)),
        scratch_shapes=[pack_stage, pltpu.SemaphoreType.DMA((6,))],
    )(a, u)
    send, normal_pair = lax.optimization_barrier((send, normal_pair))
    recv = lax.ppermute(send, "cols", partner)
    keep = pl.pallas_call(
        pack_keep_kernel, name="pack_keep", out_shape=local_shape(packed, bf16), scratch_shapes=[pack_stage]
    )(near(a), near(u))
    base = pl.pallas_call(x_kernel, name="x_terms", out_shape=local_shape(a.shape, f32))(
        near(a), near(u), near(stream_pair)
    )
    both = lax.cond(lax.axis_index("cols") % 2 == 1, along_y, along_z, keep, recv)
    other = lax.ppermute(both[rows // 2 :], "cols", partner)
    add_stage = pltpu.VMEM((16 * BACK, LANES), f32)
    base = pl.pallas_call(
        add_own_kernel, name="add_own", out_shape=local_shape(a.shape, f32), scratch_shapes=[add_stage]
    )(near(base), near(both))
    out = pl.pallas_call(
        add_other_kernel,
        name="add_other",
        out_shape=jax.ShapeDtypeStruct(a.shape, f32),
        out_specs=pl.BlockSpec(memory_space=pl.ANY),
        scratch_shapes=[add_stage, pltpu.VMEM(a.shape, f32), pltpu.SemaphoreType.DMA((3,))],
    )(near(base), near(other))
    return out.transpose(0, 2, 1, 3)


def solution(mesh):
    placed = (P(None, "cols", "rows", None), P(None, "cols", "rows", None), P(), P(), P())
    return jax.shard_map(
        local, mesh=mesh, in_specs=placed, out_specs=P(None, "cols", "rows", None), check_vma=False
    )
```

```python
import functools

import jax
import jax.numpy as jnp
from jax import lax
from jax.experimental import pallas as pl
from jax.experimental.pallas import tpu as pltpu
from jax.sharding import PartitionSpec as P

viscosity = 0.5
section_step = 0.5
LANES = 128
QUAD = 4


def pack_field(is_y, f, value, out_ref, stage, y_own, z_own):
    rows = 6 * y_own

    @pl.when(is_y)
    def _():
        for half in range(2):
            points = value(half)
            for y in range(y_own):
                stage[pl.ds(half * rows + f * y_own + y, z_own, stride=2 * rows), :] = points[y]

    @pl.when(jnp.logical_not(is_y))
    def _():
        for half in range(2):
            points = value(half).astype(jnp.bfloat16)
            for y in range(y_own):
                row = ((y // 3 * 2 + half) * 18 + f * 3 + y % 3) * z_own
                out_ref[row // 72, pl.ds(row % 72, z_own), :] = points[y]


def pack_fields(is_y, a_ref, u_ref, out_ref, stage, ready):
    for f in range(6):
        ready(f)
        ref, j = (a_ref, f) if f < 3 else (u_ref, f - 3)
        pack_field(
            is_y,
            f,
            lambda half: ref[j, :, :, pl.ds(half * LANES, LANES)].astype(jnp.float32),
            out_ref,
            stage,
            *ref.shape[1:3],
        )

    @pl.when(is_y)
    def _():
        out_ref[...] = stage[...].reshape(out_ref.shape).astype(jnp.bfloat16)


def pack_send_kernel(a_hbm, u_hbm, out_ref, a_ref, u_ref, stage, arrived):
    copies = [pltpu.make_async_copy(a_hbm.at[j], a_ref.at[j], arrived.at[j]) for j in range(3)]
    copies += [pltpu.make_async_copy(u_hbm.at[j], u_ref.at[j], arrived.at[3 + j]) for j in range(3)]
    for copy in copies:
        copy.start()
    is_y = lax.axis_index("cols") % 2 == 0
    pack_fields(is_y, a_ref, u_ref, out_ref, stage, lambda f: copies[f].wait())


def pack_keep_kernel(a_ref, u_ref, out_ref, stage):
    is_y = lax.axis_index("cols") % 2 == 1
    pack_fields(is_y, a_ref, u_ref, out_ref, stage, lambda f: None)


def x_kernel(a_ref, u_ref, px_ref, out_ref):
    comps, y_own, z_own, length = a_ref.shape
    rows = y_own * z_own
    px = px_ref[...]
    dims = (((1,), (1,)), ((), ()))
    adjoint = a_ref[...].reshape(comps * rows, length)
    a_b = adjoint.astype(jnp.bfloat16)
    u_f = u_ref[...].astype(jnp.float32).reshape(comps * rows, length)
    derivs = lax.dot_general(a_b, px, dims, preferred_element_type=jnp.float32)
    base_deriv = lax.dot_general(
        u_f.astype(jnp.bfloat16), px[:length], dims, preferred_element_type=jnp.float32
    )
    products = a_b.astype(jnp.float32) * base_deriv
    transfer = products[:rows] + products[rows : 2 * rows] + products[2 * rows :]
    u_dir = u_f[:rows]
    for c in range(comps):
        part = slice(c * rows, (c + 1) * rows)
        term = u_dir * derivs[part, :length] + viscosity * derivs[part, length:]
        if c == 0:
            term = term - transfer
        out_ref[c] = (adjoint[part] + section_step * term).reshape(y_own, z_own, length)


def z_kernel(rz_ref, pz_ref, oz_ref, derivs, base_derivs):
    chips, _, slabs, z_own = rz_ref.shape[:4]
    length = chips * 2 * z_own
    lines = [rz_ref[:, :, k].astype(jnp.float32).reshape(length, LANES) for k in range(slabs)]
    packed = [v.astype(jnp.bfloat16) for v in lines]
    pz = pz_ref[...]
    derivs[...] = jnp.dot(pz, jnp.concatenate(packed[:9], axis=1), preferred_element_type=jnp.float32)
    base_derivs[...] = jnp.dot(
        pz[:length], jnp.concatenate(packed[9:], axis=1), preferred_element_type=jnp.float32
    )
    for y in range(3):
        at = [pl.ds((3 * j + y) * LANES, LANES) for j in range(3)]
        u_dir = lines[9 + 3 * 2 + y]
        transfer = sum(lines[3 * j + y] * base_derivs[:, at[j]] for j in range(3))
        for c in range(3):
            term = u_dir * derivs[:length, at[c]] + viscosity * derivs[length:, at[c]]
            if c == 2:
                term = term - transfer
            oz_ref[:, :, 3 * c + y] = term.reshape(chips, 2, z_own, LANES).astype(jnp.bfloat16)


def y_kernel(ry_ref, py_ref, oy_ref, lines, derivs, base_derivs, terms):
    peers, rows = ry_ref.shape[:2]
    y_own = rows // 6
    length = peers * y_own
    for f in range(6):
        for p in range(peers):
            lines[f, pl.ds(p * y_own, y_own), :] = ry_ref[p, pl.ds(f * y_own, y_own), :].astype(jnp.float32)
    packed = [lines[f].astype(jnp.bfloat16) for f in range(6)]
    derivs[...] = jnp.dot(
        py_ref[...], jnp.concatenate(packed[:3], axis=1), preferred_element_type=jnp.float32
    )
    base_derivs[...] = jnp.dot(
        py_ref[pl.ds(0, length), :], jnp.concatenate(packed[3:], axis=1), preferred_element_type=jnp.float32
    )
    block = 48
    for b in range(length // block):
        at = pl.ds(b * block, block)
        lane = [pl.ds(j * LANES, LANES) for j in range(3)]
        u_dir = lines[4, at, :]
        transfer = sum(lines[j, at, :] * base_derivs[at, lane[j]] for j in range(3))
        for c in range(3):
            term = u_dir * derivs[at, lane[c]] + viscosity * derivs[pl.ds(length + b * block, block), lane[c]]
            if c == 1:
                term = term - transfer
            terms[c, at, :] = term
    for p in range(peers):
        parts = [terms[c, pl.ds(p * y_own, y_own), :] for c in range(3)]
        oy_ref[p] = jnp.concatenate(parts, axis=0).reshape(oy_ref.shape[1:]).astype(jnp.bfloat16)


def order_kernel(rz_ref, out_ref):
    pieces, _, slabs, z_own = rz_ref.shape[:4]
    quads = out_ref.shape[1]
    for side in range(2):
        for p in range(pieces):
            for k in range(slabs):
                value = rz_ref[p, side, k].astype(jnp.float32)
                for part in range(2):
                    quad = (p * slabs + k) * 2 + part
                    out_ref[16 * side + quad // quads, quad % quads] = value[QUAD * part : QUAD * (part + 1)].astype(
                        jnp.bfloat16
                    )


def add_parts(is_y, base_ref, part_ref, out_ref, stage, done):
    comps, y_own, z_own, _ = base_ref.shape
    quads = part_ref.shape[1]
    pitch = quads * QUAD

    @pl.when(is_y)
    def _():
        stage[...] = part_ref[pl.ds(0, 16)].astype(jnp.float32).reshape(stage.shape)

    for c in range(comps):

        @pl.when(is_y)
        def _():
            for y in range(y_own):
                for half in range(2):
                    at = pl.ds(half * LANES, LANES)
                    piece = stage[pl.ds(half * pitch + c * y_own + y, z_own, stride=2 * pitch), :]
                    out_ref[c, y, :, at] = base_ref[c, y, :, at] + section_step * piece

        @pl.when(jnp.logical_not(is_y))
        def _():
            for y in range(y_own):
                for half in range(2):
                    at = pl.ds(half * LANES, LANES)
                    quad = ((y // 3 * 2 + half) * 9 + c * 3 + y % 3) * 2
                    piece = jnp.concatenate(
                        [part_ref[at_q // quads, at_q % quads].astype(jnp.float32) for at_q in (quad, quad + 1)], axis=0
                    )
                    out_ref[c, y, :, at] = base_ref[c, y, :, at] + section_step * piece

        done(c)


def add_own_kernel(base_ref, part_ref, out_ref, stage):
    is_y = lax.axis_index("cols") % 2 == 1
    add_parts(is_y, base_ref, part_ref, out_ref, stage, lambda c: None)


def add_other_kernel(base_ref, part_ref, out_hbm, stage, total, left):
    is_y = lax.axis_index("cols") % 2 == 0
    copies = [pltpu.make_async_copy(total.at[c], out_hbm.at[c], left.at[c]) for c in range(3)]
    add_parts(is_y, base_ref, part_ref, total, stage, lambda c: copies[c].start())
    for copy in copies:
        copy.wait()


def local(adjoint, base_flow, stream_pair, normal_pair, span_pair):
    f32, bf16 = jnp.float32, jnp.bfloat16
    rows = lax.axis_size("rows")
    cols = lax.axis_size("cols")
    chips = cols // 2
    _, z_own, y_own, length_x = adjoint.shape
    length_y = rows * y_own
    length_z = cols * z_own
    a = adjoint.transpose(0, 2, 1, 3)
    u = base_flow.transpose(0, 2, 1, 3)
    local_shape = pltpu.VMEM
    near = functools.partial(pltpu.with_memory_space_constraint, memory_space=pltpu.VMEM)
    exchange = functools.partial(lax.all_to_all, split_axis=0, concat_axis=0, tiled=True)
    partner = [(i, i ^ 1) for i in range(cols)]
    alike = [list(range(core, cols, 2)) for core in range(2)]

    def along_y(keep, recv):
        lines = exchange(jnp.concatenate([keep, recv], axis=0), "rows")
        terms = pl.pallas_call(
            y_kernel,
            name="y_terms",
            out_shape=local_shape((rows, 3 * y_own // QUAD, QUAD, LANES), bf16),
            scratch_shapes=[
                pltpu.VMEM((6, length_y, LANES), f32),
                pltpu.VMEM((2 * length_y, 3 * LANES), f32),
                pltpu.VMEM((length_y, 3 * LANES), f32),
                pltpu.VMEM((3, length_y, LANES), f32),
            ],
        )(near(lines), near(normal_pair))
        return exchange(terms, "rows")

    def along_z(keep, recv):
        pair = [part.reshape(chips, 1, 18, z_own, LANES) for part in (keep, recv)]
        lines = exchange(jnp.concatenate(pair, axis=1), "cols", axis_index_groups=alike)
        terms = pl.pallas_call(
            z_kernel,
            name="z_terms",
            out_shape=local_shape((chips, 2, 9, z_own, LANES), bf16),
            scratch_shapes=[
                pltpu.VMEM((2 * length_z, 9 * LANES), f32),
                pltpu.VMEM((length_z, 9 * LANES), f32),
            ],
        )(near(lines), near(span_pair))
        back = exchange(terms, "cols", axis_index_groups=alike)
        ordered = pl.pallas_call(
            order_kernel, name="order_z", out_shape=local_shape((rows, 3 * y_own // QUAD, QUAD, LANES), bf16)
        )(near(back))
        return ordered

    packed = (2 * z_own, 6 * y_own, LANES)
    pack_stage = pltpu.VMEM((2 * z_own * 6 * y_own, LANES), f32)
    send, a, u = pl.pallas_call(
        pack_send_kernel,
        name="pack_send",
        in_specs=[pl.BlockSpec(memory_space=pl.ANY)] * 2,
        out_shape=(local_shape(packed, bf16), local_shape(a.shape, f32), local_shape(u.shape, bf16)),
        scratch_shapes=[pack_stage, pltpu.SemaphoreType.DMA((6,))],
    )(a, u)
    send, normal_pair = lax.optimization_barrier((send, normal_pair))
    recv = lax.ppermute(send, "cols", partner)
    keep = pl.pallas_call(
        pack_keep_kernel, name="pack_keep", out_shape=local_shape(packed, bf16), scratch_shapes=[pack_stage]
    )(near(a), near(u))
    base = pl.pallas_call(x_kernel, name="x_terms", out_shape=local_shape(a.shape, f32))(
        near(a), near(u), near(stream_pair)
    )
    both = lax.cond(lax.axis_index("cols") % 2 == 1, along_y, along_z, keep, recv)
    other = lax.ppermute(both[rows // 2 :], "cols", partner)
    add_stage = pltpu.VMEM((16 * 3 * y_own, LANES), f32)
    base = pl.pallas_call(
        add_own_kernel, name="add_own", out_shape=local_shape(a.shape, f32), scratch_shapes=[add_stage]
    )(near(base), near(both))
    out = pl.pallas_call(
        add_other_kernel,
        name="add_other",
        out_shape=jax.ShapeDtypeStruct(a.shape, f32),
        out_specs=pl.BlockSpec(memory_space=pl.ANY),
        scratch_shapes=[add_stage, pltpu.VMEM(a.shape, f32), pltpu.SemaphoreType.DMA((3,))],
    )(near(base), near(other))
    return out.transpose(0, 2, 1, 3)


def solution(mesh):
    placed = (P(None, "cols", "rows", None), P(None, "cols", "rows", None), P(), P(), P())
    return jax.shard_map(
        local, mesh=mesh, in_specs=placed, out_specs=P(None, "cols", "rows", None), check_vma=False
    )
```

```python
import functools

import jax
import jax.numpy as jnp
from jax import lax
from jax.experimental import pallas as pl
from jax.experimental.pallas import tpu as pltpu
from jax.sharding import PartitionSpec as P

viscosity = 0.5
section_step = 0.5
LANES = 128
QUAD = 4


def pack_field(is_y, f, value, out_ref, stage, y_own, z_own):
    rows = 6 * y_own

    @pl.when(is_y)
    def _():
        for half in range(2):
            points = value(half)
            for y in range(y_own):
                stage[pl.ds(half * rows + f * y_own + y, z_own, stride=2 * rows), :] = points[y]

    @pl.when(jnp.logical_not(is_y))
    def _():
        for half in range(2):
            points = value(half).astype(jnp.bfloat16)
            for y in range(y_own):
                row = ((y // 3 * 2 + half) * 18 + f * 3 + y % 3) * z_own
                out_ref[row // 72, pl.ds(row % 72, z_own), :] = points[y]


def pack_fields(is_y, a_ref, u_ref, out_ref, stage, ready):
    for f in range(6):
        ready(f)
        ref, j = (a_ref, f) if f < 3 else (u_ref, f - 3)
        pack_field(
            is_y,
            f,
            lambda half: ref[j, :, :, pl.ds(half * LANES, LANES)].astype(jnp.float32),
            out_ref,
            stage,
            *ref.shape[1:3],
        )

    @pl.when(is_y)
    def _():
        out_ref[...] = stage[...].reshape(out_ref.shape).astype(jnp.bfloat16)


def pack_send_kernel(a_hbm, u_hbm, out_ref, a_ref, u_ref, stage, arrived):
    copies = [pltpu.make_async_copy(a_hbm.at[j], a_ref.at[j], arrived.at[j]) for j in range(3)]
    copies += [pltpu.make_async_copy(u_hbm.at[j], u_ref.at[j], arrived.at[3 + j]) for j in range(3)]
    for copy in copies:
        copy.start()
    is_y = lax.axis_index("cols") % 2 == 0
    pack_fields(is_y, a_ref, u_ref, out_ref, stage, lambda f: copies[f].wait())


def pack_keep_kernel(a_ref, u_ref, out_ref, stage):
    is_y = lax.axis_index("cols") % 2 == 1
    pack_fields(is_y, a_ref, u_ref, out_ref, stage, lambda f: None)


def x_kernel(a_ref, u_ref, px_ref, out_ref):
    comps, y_own, z_own, length = a_ref.shape
    rows = y_own * z_own
    px = px_ref[...]
    dims = (((1,), (1,)), ((), ()))
    adjoint = a_ref[...].reshape(comps * rows, length)
    a_b = adjoint.astype(jnp.bfloat16)
    u_f = u_ref[...].astype(jnp.float32).reshape(comps * rows, length)
    derivs = lax.dot_general(a_b, px, dims, preferred_element_type=jnp.float32)
    base_deriv = lax.dot_general(
        u_f.astype(jnp.bfloat16), px[:length], dims, preferred_element_type=jnp.float32
    )
    products = a_b.astype(jnp.float32) * base_deriv
    transfer = products[:rows] + products[rows : 2 * rows] + products[2 * rows :]
    u_dir = u_f[:rows]
    for c in range(comps):
        part = slice(c * rows, (c + 1) * rows)
        term = u_dir * derivs[part, :length] + viscosity * derivs[part, length:]
        if c == 0:
            term = term - transfer
        out_ref[c] = (adjoint[part] + section_step * term).reshape(y_own, z_own, length)


def z_kernel(rz_ref, pz_ref, oz_ref, derivs, base_derivs):
    chips, _, slabs, z_own = rz_ref.shape[:4]
    length = chips * 2 * z_own
    lines = [rz_ref[:, :, k].astype(jnp.float32).reshape(length, LANES) for k in range(slabs)]
    packed = [v.astype(jnp.bfloat16) for v in lines]
    pz = pz_ref[...]
    derivs[...] = jnp.dot(pz, jnp.concatenate(packed[:9], axis=1), preferred_element_type=jnp.float32)
    base_derivs[...] = jnp.dot(
        pz[:length], jnp.concatenate(packed[9:], axis=1), preferred_element_type=jnp.float32
    )
    for y in range(3):
        at = [pl.ds((3 * j + y) * LANES, LANES) for j in range(3)]
        u_dir = lines[9 + 3 * 2 + y]
        transfer = sum(lines[3 * j + y] * base_derivs[:, at[j]] for j in range(3))
        for c in range(3):
            term = u_dir * derivs[:length, at[c]] + viscosity * derivs[length:, at[c]]
            if c == 2:
                term = term - transfer
            oz_ref[:, :, 3 * c + y] = term.reshape(chips, 2, z_own, LANES).astype(jnp.bfloat16)


def y_kernel(ry_ref, py_ref, oy_ref, lines, first, second, terms):
    peers, rows = ry_ref.shape[:2]
    y_own = rows // 6
    length = peers * y_own
    for f in range(6):
        for p in range(peers):
            lines[f, pl.ds(p * y_own, y_own), :] = ry_ref[p, pl.ds(f * y_own, y_own), :].astype(jnp.float32)
    packed = [lines[f].astype(jnp.bfloat16) for f in range(6)]
    first[...] = jnp.dot(
        py_ref[pl.ds(0, length), :], jnp.concatenate(packed, axis=1), preferred_element_type=jnp.float32
    )
    second[...] = jnp.dot(
        py_ref[pl.ds(length, length), :], jnp.concatenate(packed[:3], axis=1), preferred_element_type=jnp.float32
    )
    block = 48
    for b in range(length // block):
        at = pl.ds(b * block, block)
        lane = [pl.ds(j * LANES, LANES) for j in range(6)]
        u_dir = lines[4, at, :]
        transfer = sum(lines[j, at, :] * first[at, lane[3 + j]] for j in range(3))
        for c in range(3):
            term = u_dir * first[at, lane[c]] + viscosity * second[at, lane[c]]
            if c == 1:
                term = term - transfer
            terms[c, at, :] = term
    for p in range(peers):
        parts = [terms[c, pl.ds(p * y_own, y_own), :] for c in range(3)]
        oy_ref[p] = jnp.concatenate(parts, axis=0).reshape(oy_ref.shape[1:]).astype(jnp.bfloat16)


def order_kernel(rz_ref, out_ref):
    pieces, _, slabs, z_own = rz_ref.shape[:4]
    quads = out_ref.shape[1]
    for side in range(2):
        for p in range(pieces):
            for k in range(slabs):
                value = rz_ref[p, side, k].astype(jnp.float32)
                for part in range(2):
                    quad = (p * slabs + k) * 2 + part
                    out_ref[16 * side + quad // quads, quad % quads] = value[QUAD * part : QUAD * (part + 1)].astype(
                        jnp.bfloat16
                    )


def add_parts(is_y, base_ref, part_ref, out_ref, stage, done):
    comps, y_own, z_own, _ = base_ref.shape
    quads = part_ref.shape[1]
    pitch = quads * QUAD

    @pl.when(is_y)
    def _():
        stage[...] = part_ref[pl.ds(0, 16)].astype(jnp.float32).reshape(stage.shape)

    for c in range(comps):

        @pl.when(is_y)
        def _():
            for y in range(y_own):
                for half in range(2):
                    at = pl.ds(half * LANES, LANES)
                    piece = stage[pl.ds(half * pitch + c * y_own + y, z_own, stride=2 * pitch), :]
                    out_ref[c, y, :, at] = base_ref[c, y, :, at] + section_step * piece

        @pl.when(jnp.logical_not(is_y))
        def _():
            for y in range(y_own):
                for half in range(2):
                    at = pl.ds(half * LANES, LANES)
                    quad = ((y // 3 * 2 + half) * 9 + c * 3 + y % 3) * 2
                    piece = jnp.concatenate(
                        [part_ref[at_q // quads, at_q % quads].astype(jnp.float32) for at_q in (quad, quad + 1)], axis=0
                    )
                    out_ref[c, y, :, at] = base_ref[c, y, :, at] + section_step * piece

        done(c)


def add_own_kernel(base_ref, part_ref, out_ref, stage):
    is_y = lax.axis_index("cols") % 2 == 1
    add_parts(is_y, base_ref, part_ref, out_ref, stage, lambda c: None)


def add_other_kernel(base_ref, part_ref, out_hbm, stage, total, left):
    is_y = lax.axis_index("cols") % 2 == 0
    copies = [pltpu.make_async_copy(total.at[c], out_hbm.at[c], left.at[c]) for c in range(3)]
    add_parts(is_y, base_ref, part_ref, total, stage, lambda c: copies[c].start())
    for copy in copies:
        copy.wait()


def local(adjoint, base_flow, stream_pair, normal_pair, span_pair):
    f32, bf16 = jnp.float32, jnp.bfloat16
    rows = lax.axis_size("rows")
    cols = lax.axis_size("cols")
    chips = cols // 2
    _, z_own, y_own, length_x = adjoint.shape
    length_y = rows * y_own
    length_z = cols * z_own
    a = adjoint.transpose(0, 2, 1, 3)
    u = base_flow.transpose(0, 2, 1, 3)
    local_shape = pltpu.VMEM
    near = functools.partial(pltpu.with_memory_space_constraint, memory_space=pltpu.VMEM)
    exchange = functools.partial(lax.all_to_all, split_axis=0, concat_axis=0, tiled=True)
    partner = [(i, i ^ 1) for i in range(cols)]
    alike = [list(range(core, cols, 2)) for core in range(2)]

    def along_y(keep, recv):
        lines = exchange(jnp.concatenate([keep, recv], axis=0), "rows")
        terms = pl.pallas_call(
            y_kernel,
            name="y_terms",
            out_shape=local_shape((rows, 3 * y_own // QUAD, QUAD, LANES), bf16),
            scratch_shapes=[
                pltpu.VMEM((6, length_y, LANES), f32),
                pltpu.VMEM((length_y, 6 * LANES), f32),
                pltpu.VMEM((length_y, 3 * LANES), f32),
                pltpu.VMEM((3, length_y, LANES), f32),
            ],
        )(near(lines), near(normal_pair))
        return exchange(terms, "rows")

    def along_z(keep, recv):
        pair = [part.reshape(chips, 1, 18, z_own, LANES) for part in (keep, recv)]
        lines = exchange(jnp.concatenate(pair, axis=1), "cols", axis_index_groups=alike)
        terms = pl.pallas_call(
            z_kernel,
            name="z_terms",
            out_shape=local_shape((chips, 2, 9, z_own, LANES), bf16),
            scratch_shapes=[
                pltpu.VMEM((2 * length_z, 9 * LANES), f32),
                pltpu.VMEM((length_z, 9 * LANES), f32),
            ],
        )(near(lines), near(span_pair))
        back = exchange(terms, "cols", axis_index_groups=alike)
        ordered = pl.pallas_call(
            order_kernel, name="order_z", out_shape=local_shape((rows, 3 * y_own // QUAD, QUAD, LANES), bf16)
        )(near(back))
        return ordered

    packed = (2 * z_own, 6 * y_own, LANES)
    pack_stage = pltpu.VMEM((2 * z_own * 6 * y_own, LANES), f32)
    send, a, u = pl.pallas_call(
        pack_send_kernel,
        name="pack_send",
        in_specs=[pl.BlockSpec(memory_space=pl.ANY)] * 2,
        out_shape=(local_shape(packed, bf16), local_shape(a.shape, f32), local_shape(u.shape, bf16)),
        scratch_shapes=[pack_stage, pltpu.SemaphoreType.DMA((6,))],
    )(a, u)
    send, normal_pair = lax.optimization_barrier((send, normal_pair))
    recv = lax.ppermute(send, "cols", partner)
    keep = pl.pallas_call(
        pack_keep_kernel, name="pack_keep", out_shape=local_shape(packed, bf16), scratch_shapes=[pack_stage]
    )(near(a), near(u))
    base = pl.pallas_call(x_kernel, name="x_terms", out_shape=local_shape(a.shape, f32))(
        near(a), near(u), near(stream_pair)
    )
    both = lax.cond(lax.axis_index("cols") % 2 == 1, along_y, along_z, keep, recv)
    other = lax.ppermute(both[rows // 2 :], "cols", partner)
    add_stage = pltpu.VMEM((16 * 3 * y_own, LANES), f32)
    base = pl.pallas_call(
        add_own_kernel, name="add_own", out_shape=local_shape(a.shape, f32), scratch_shapes=[add_stage]
    )(near(base), near(both))
    out = pl.pallas_call(
        add_other_kernel,
        name="add_other",
        out_shape=jax.ShapeDtypeStruct(a.shape, f32),
        out_specs=pl.BlockSpec(memory_space=pl.ANY),
        scratch_shapes=[add_stage, pltpu.VMEM(a.shape, f32), pltpu.SemaphoreType.DMA((3,))],
    )(near(base), near(other))
    return out.transpose(0, 2, 1, 3)


def solution(mesh):
    placed = (P(None, "cols", "rows", None), P(None, "cols", "rows", None), P(), P(), P())
    return jax.shard_map(
        local, mesh=mesh, in_specs=placed, out_specs=P(None, "cols", "rows", None), check_vma=False
    )
```

```python
import functools

import jax
import jax.numpy as jnp
from jax import lax
from jax.experimental import pallas as pl
from jax.experimental.pallas import tpu as pltpu
from jax.sharding import PartitionSpec as P

viscosity = 0.5
section_step = 0.5
LANES = 128
QUAD = 4


def pack_field(is_y, f, value, out_ref, stage, y_own, z_own):
    rows = 6 * y_own

    @pl.when(is_y)
    def _():
        for half in range(2):
            points = value(half)
            for y in range(y_own):
                stage[pl.ds(half * rows + f * y_own + y, z_own, stride=2 * rows), :] = points[y]

    @pl.when(jnp.logical_not(is_y))
    def _():
        for half in range(2):
            points = value(half).astype(jnp.bfloat16)
            for y in range(y_own):
                row = ((y // 3 * 2 + half) * 18 + f * 3 + y % 3) * z_own
                out_ref[row // 72, pl.ds(row % 72, z_own), :] = points[y]


def pack_fields(is_y, a_ref, u_ref, out_ref, stage, ready):
    for f in range(6):
        ready(f)
        ref, j = (a_ref, f) if f < 3 else (u_ref, f - 3)
        pack_field(
            is_y,
            f,
            lambda half: ref[j, :, :, pl.ds(half * LANES, LANES)].astype(jnp.float32),
            out_ref,
            stage,
            *ref.shape[1:3],
        )

    @pl.when(is_y)
    def _():
        out_ref[...] = stage[...].reshape(out_ref.shape).astype(jnp.bfloat16)


def pack_send_kernel(a_hbm, u_hbm, out_ref, a_ref, u_ref, stage, arrived):
    copies = [pltpu.make_async_copy(a_hbm.at[j], a_ref.at[j], arrived.at[j]) for j in range(3)]
    copies += [pltpu.make_async_copy(u_hbm.at[j], u_ref.at[j], arrived.at[3 + j]) for j in range(3)]
    for copy in copies:
        copy.start()
    is_y = lax.axis_index("cols") % 2 == 0
    pack_fields(is_y, a_ref, u_ref, out_ref, stage, lambda f: copies[f].wait())


def pack_keep_kernel(a_ref, u_ref, out_ref, stage):
    is_y = lax.axis_index("cols") % 2 == 1
    pack_fields(is_y, a_ref, u_ref, out_ref, stage, lambda f: None)


def x_kernel(a_ref, u_ref, px_ref, out_ref):
    comps, y_own, z_own, length = a_ref.shape
    rows = y_own * z_own
    px = px_ref[...]
    dims = (((1,), (1,)), ((), ()))
    adjoint = a_ref[...].reshape(comps * rows, length)
    a_b = adjoint.astype(jnp.bfloat16)
    u_f = u_ref[...].astype(jnp.float32).reshape(comps * rows, length)
    derivs = lax.dot_general(a_b, px, dims, preferred_element_type=jnp.float32)
    base_deriv = lax.dot_general(
        u_f.astype(jnp.bfloat16), px[:length], dims, preferred_element_type=jnp.float32
    )
    products = a_b.astype(jnp.float32) * base_deriv
    transfer = products[:rows] + products[rows : 2 * rows] + products[2 * rows :]
    u_dir = u_f[:rows]
    for c in range(comps):
        part = slice(c * rows, (c + 1) * rows)
        term = u_dir * derivs[part, :length] + viscosity * derivs[part, length:]
        if c == 0:
            term = term - transfer
        out_ref[c] = (adjoint[part] + section_step * term).reshape(y_own, z_own, length)


def z_kernel(rz_ref, pz_ref, oz_ref, derivs, base_derivs):
    chips, _, slabs, z_own = rz_ref.shape[:4]
    length = chips * 2 * z_own
    lines = [rz_ref[:, :, k].astype(jnp.float32).reshape(length, LANES) for k in range(slabs)]
    packed = [v.astype(jnp.bfloat16) for v in lines]
    pz = pz_ref[...]
    derivs[...] = jnp.dot(pz, jnp.concatenate(packed[:9], axis=1), preferred_element_type=jnp.float32)
    base_derivs[...] = jnp.dot(
        pz[:length], jnp.concatenate(packed[9:], axis=1), preferred_element_type=jnp.float32
    )
    for y in range(3):
        at = [pl.ds((3 * j + y) * LANES, LANES) for j in range(3)]
        u_dir = lines[9 + 3 * 2 + y]
        transfer = sum(lines[3 * j + y] * base_derivs[:, at[j]] for j in range(3))
        for c in range(3):
            term = u_dir * derivs[:length, at[c]] + viscosity * derivs[length:, at[c]]
            if c == 2:
                term = term - transfer
            oz_ref[:, :, 3 * c + y] = term.reshape(chips, 2, z_own, LANES).astype(jnp.bfloat16)


def y_kernel(ry_ref, py_ref, oy_ref, lines, first, second):
    peers, rows = ry_ref.shape[:2]
    y_own = rows // 6
    length = peers * y_own
    for f in range(6):
        for p in range(peers):
            lines[f, pl.ds(p * y_own, y_own), :] = ry_ref[p, pl.ds(f * y_own, y_own), :].astype(jnp.float32)
    packed = [lines[f].astype(jnp.bfloat16) for f in range(6)]
    first[...] = jnp.dot(
        py_ref[pl.ds(0, length), :], jnp.concatenate(packed, axis=1), preferred_element_type=jnp.float32
    )
    second[...] = jnp.dot(
        py_ref[pl.ds(length, length), :], jnp.concatenate(packed[:3], axis=1), preferred_element_type=jnp.float32
    )
    block = 2 * y_own
    for b in range(length // block):
        at = pl.ds(b * block, block)
        lane = [pl.ds(j * LANES, LANES) for j in range(6)]
        u_dir = lines[4, at, :]
        transfer = sum(lines[j, at, :] * first[at, lane[3 + j]] for j in range(3))
        terms = [u_dir * first[at, lane[c]] + viscosity * second[at, lane[c]] for c in range(3)]
        terms[1] = terms[1] - transfer
        for p in range(2):
            parts = [term[p * y_own : (p + 1) * y_own] for term in terms]
            oy_ref[2 * b + p] = jnp.concatenate(parts, axis=0).reshape(oy_ref.shape[1:]).astype(jnp.bfloat16)


def order_kernel(rz_ref, out_ref):
    pieces, _, slabs, z_own = rz_ref.shape[:4]
    quads = out_ref.shape[1]
    for side in range(2):
        for p in range(pieces):
            for k in range(slabs):
                value = rz_ref[p, side, k].astype(jnp.float32)
                for part in range(2):
                    quad = (p * slabs + k) * 2 + part
                    out_ref[16 * side + quad // quads, quad % quads] = value[QUAD * part : QUAD * (part + 1)].astype(
                        jnp.bfloat16
                    )


def add_parts(is_y, base_ref, part_ref, out_ref, stage, done):
    comps, y_own, z_own, _ = base_ref.shape
    quads = part_ref.shape[1]
    pitch = quads * QUAD

    @pl.when(is_y)
    def _():
        stage[...] = part_ref[pl.ds(0, 16)].astype(jnp.float32).reshape(stage.shape)

    for c in range(comps):

        @pl.when(is_y)
        def _():
            for y in range(y_own):
                for half in range(2):
                    at = pl.ds(half * LANES, LANES)
                    piece = stage[pl.ds(half * pitch + c * y_own + y, z_own, stride=2 * pitch), :]
                    out_ref[c, y, :, at] = base_ref[c, y, :, at] + section_step * piece

        @pl.when(jnp.logical_not(is_y))
        def _():
            for y in range(y_own):
                for half in range(2):
                    at = pl.ds(half * LANES, LANES)
                    quad = ((y // 3 * 2 + half) * 9 + c * 3 + y % 3) * 2
                    piece = jnp.concatenate(
                        [part_ref[at_q // quads, at_q % quads].astype(jnp.float32) for at_q in (quad, quad + 1)], axis=0
                    )
                    out_ref[c, y, :, at] = base_ref[c, y, :, at] + section_step * piece

        done(c)


def add_own_kernel(base_ref, part_ref, out_ref, stage):
    is_y = lax.axis_index("cols") % 2 == 1
    add_parts(is_y, base_ref, part_ref, out_ref, stage, lambda c: None)


def add_other_kernel(base_ref, part_ref, out_hbm, stage, total, left):
    is_y = lax.axis_index("cols") % 2 == 0
    copies = [pltpu.make_async_copy(total.at[c], out_hbm.at[c], left.at[c]) for c in range(3)]
    add_parts(is_y, base_ref, part_ref, total, stage, lambda c: copies[c].start())
    for copy in copies:
        copy.wait()


def local(adjoint, base_flow, stream_pair, normal_pair, span_pair):
    f32, bf16 = jnp.float32, jnp.bfloat16
    rows = lax.axis_size("rows")
    cols = lax.axis_size("cols")
    chips = cols // 2
    _, z_own, y_own, length_x = adjoint.shape
    length_y = rows * y_own
    length_z = cols * z_own
    a = adjoint.transpose(0, 2, 1, 3)
    u = base_flow.transpose(0, 2, 1, 3)
    local_shape = pltpu.VMEM
    near = functools.partial(pltpu.with_memory_space_constraint, memory_space=pltpu.VMEM)
    exchange = functools.partial(lax.all_to_all, split_axis=0, concat_axis=0, tiled=True)
    partner = [(i, i ^ 1) for i in range(cols)]
    alike = [list(range(core, cols, 2)) for core in range(2)]

    def along_y(keep, recv):
        lines = exchange(jnp.concatenate([keep, recv], axis=0), "rows")
        terms = pl.pallas_call(
            y_kernel,
            name="y_terms",
            out_shape=local_shape((rows, 3 * y_own // QUAD, QUAD, LANES), bf16),
            scratch_shapes=[
                pltpu.VMEM((6, length_y, LANES), f32),
                pltpu.VMEM((length_y, 6 * LANES), f32),
                pltpu.VMEM((length_y, 3 * LANES), f32),
            ],
        )(near(lines), near(normal_pair))
        return exchange(terms, "rows")

    def along_z(keep, recv):
        pair = [part.reshape(chips, 1, 18, z_own, LANES) for part in (keep, recv)]
        lines = exchange(jnp.concatenate(pair, axis=1), "cols", axis_index_groups=alike)
        terms = pl.pallas_call(
            z_kernel,
            name="z_terms",
            out_shape=local_shape((chips, 2, 9, z_own, LANES), bf16),
            scratch_shapes=[
                pltpu.VMEM((2 * length_z, 9 * LANES), f32),
                pltpu.VMEM((length_z, 9 * LANES), f32),
            ],
        )(near(lines), near(span_pair))
        back = exchange(terms, "cols", axis_index_groups=alike)
        ordered = pl.pallas_call(
            order_kernel, name="order_z", out_shape=local_shape((rows, 3 * y_own // QUAD, QUAD, LANES), bf16)
        )(near(back))
        return ordered

    packed = (2 * z_own, 6 * y_own, LANES)
    pack_stage = pltpu.VMEM((2 * z_own * 6 * y_own, LANES), f32)
    send, a, u = pl.pallas_call(
        pack_send_kernel,
        name="pack_send",
        in_specs=[pl.BlockSpec(memory_space=pl.ANY)] * 2,
        out_shape=(local_shape(packed, bf16), local_shape(a.shape, f32), local_shape(u.shape, bf16)),
        scratch_shapes=[pack_stage, pltpu.SemaphoreType.DMA((6,))],
    )(a, u)
    send, normal_pair = lax.optimization_barrier((send, normal_pair))
    recv = lax.ppermute(send, "cols", partner)
    keep = pl.pallas_call(
        pack_keep_kernel, name="pack_keep", out_shape=local_shape(packed, bf16), scratch_shapes=[pack_stage]
    )(near(a), near(u))
    base = pl.pallas_call(x_kernel, name="x_terms", out_shape=local_shape(a.shape, f32))(
        near(a), near(u), near(stream_pair)
    )
    both = lax.cond(lax.axis_index("cols") % 2 == 1, along_y, along_z, keep, recv)
    other = lax.ppermute(both[rows // 2 :], "cols", partner)
    add_stage = pltpu.VMEM((16 * 3 * y_own, LANES), f32)
    base = pl.pallas_call(
        add_own_kernel, name="add_own", out_shape=local_shape(a.shape, f32), scratch_shapes=[add_stage]
    )(near(base), near(both))
    out = pl.pallas_call(
        add_other_kernel,
        name="add_other",
        out_shape=jax.ShapeDtypeStruct(a.shape, f32),
        out_specs=pl.BlockSpec(memory_space=pl.ANY),
        scratch_shapes=[add_stage, pltpu.VMEM(a.shape, f32), pltpu.SemaphoreType.DMA((3,))],
    )(near(base), near(other))
    return out.transpose(0, 2, 1, 3)


def solution(mesh):
    placed = (P(None, "cols", "rows", None), P(None, "cols", "rows", None), P(), P(), P())
    return jax.shard_map(
        local, mesh=mesh, in_specs=placed, out_specs=P(None, "cols", "rows", None), check_vma=False
    )
```
